32 devices in a mesh: layer: 8 (over z, x), lat: 4 (over y, core).
Axes of the slice: x: 2, y: 2, z: 4, core: 2. Of those that a mesh axis runs over, the one named last changes fastest.
Arguments:
- inverse: bfloat16 [8, 8, 512, 512], P('layer', 'lat')
- tiles: bfloat16 [1024, 256], P(('layer', 'lat')), may hold values from -6 to 6
- tile_dest: int32 [1024, 1], P(('layer', 'lat')), may hold values from 0 to 31; in each aligned block of 32 rows (0 to 31, 32 to 63, ...) at most 2 rows name the same one
- tile_code: int32 [1024], P(('layer', 'lat')), may hold values from 0 to 31
Outputs:
- solution: float32 [8, 8, 8, 512], P('layer', 'lat')
The draws below stay inside these ranges and needn't reach their ends.
Inputs may be any that keep to these rules, and one draw needn't show every extreme that they name: `tile_dest`: the rows of one device name any one device at most 2 times; in every draw some device's rows name some device exactly 2 times.
All inputs are finite; a program needn't handle non-finite values.
Results may differ from the reference program's by a relative error of at most 0.004.
Values may be sent and summed in bfloat16 or wider, within the bound.
A program may use at most 128 MiB of HBM per device.

```python
import math
import jax
import jax.numpy as jnp
import numpy as np
from jax import lax

BLOCK = 128
DEP = 2
SRC = 8
NB = 2
CAP = 2
M = 512
BLOCKS = 8
TPD = 32
TILES = 1024
N_LAYER = 8
N_LAT = 4


def draw_inverse(key, part):
    entire_extent = (N_LAYER, NB * N_LAT, M, M)
    trace_len = 2 * BLOCK
    far_rows = trace_len * (DEP - 1)
    perturbation_seed, principal_seed, damping_seed, spike_seed, surviving_seed = jax.random.split(key, 5)
    row_at = lax.broadcasted_iota(jnp.int32, entire_extent, 2)
    col_at = lax.broadcasted_iota(jnp.int32, entire_extent, 3)
    noise = jax.random.normal(perturbation_seed, entire_extent, jnp.float32) * (0.3 / math.sqrt(M))
    diagonal = jax.random.uniform(principal_seed, entire_extent, jnp.float32, 0.8, 1.6)
    low_rate = 0.5 / N_LAYER
    high_rate = 2.0
    damping_multiplier = jnp.exp(jax.random.uniform(damping_seed, entire_extent, jnp.float32, math.log(low_rate), math.log(high_rate)))
    spike_occurrences = jax.random.uniform(spike_seed, entire_extent, jnp.float32) < 3.0 / N_LAYER
    surviving_proportion = jax.random.uniform(surviving_seed, entire_extent, jnp.float32, 0.5, 0.8)
    leftover_amount = jnp.exp(-damping_multiplier) * jnp.where(spike_occurrences, surviving_proportion, 1.0)
    lower_band = (row_at >= far_rows) & (col_at == row_at - far_rows)
    upper_band = (row_at < trace_len) & (col_at == row_at + far_rows)
    entries = noise + jnp.where(row_at == col_at, diagonal, 0.0) + jnp.where(lower_band | upper_band, leftover_amount, 0.0)
    return entries.astype(jnp.bfloat16)


def touch_ends(values, own_key, smallest, high):
    spot = [jax.random.randint(jax.random.fold_in(own_key, axis), (), 0, length) for axis, length in enumerate(values.shape)]
    longest = values.shape.index(max(values.shape))
    next_to = spot[:longest] + [(spot[longest] + 1) % values.shape[longest]] + spot[longest + 1:]
    return values.at[tuple(spot)].set(smallest).at[tuple(next_to)].set(high)


def block_levels(rng, shape, cuts, low, high):
    gain, own = 1.0, jax.random.fold_in(rng, 6)
    for position, shards_of in cuts:
        heights = jnp.exp(jax.random.uniform(jax.random.fold_in(own, position), (shards_of,), jnp.float32, low / len(cuts), high / len(cuts)))
        gain = gain * jnp.repeat(heights, shape[position] // shards_of).reshape([-1 if axis == position else 1 for axis in range(len(shape))])
    return gain


def assign_block(stream_key, own, number, rows, amount, top, reach, slope):
    order = jax.random.permutation(stream_key, amount)
    heavy_load, usual = shares(amount, rows * top, reach, slope, True), shares(amount, rows * top, reach, slope, False)
    places = jnp.arange(amount)

    def named(tallies, rotation):
        used = int((tallies > 0).sum())
        fixed = max(1, used // 4)
        shifted = fixed + (places - fixed + rotation * (used - fixed)) % max(1, amount - fixed)
        return jnp.zeros((amount,), jnp.int32).at[order[jnp.where(places < fixed, places, shifted)]].set(jnp.asarray(tallies, jnp.int32))

    tallies = jnp.where(number % 4 == 0, named(heavy_load, number // 4), named(usual, number - number // 4 - 1))
    mixed = jax.random.permutation(jax.random.fold_in(own, 3), amount)
    source_of, sink = mixed[0:amount // 2 * 2:2], mixed[1:amount // 2 * 2:2]
    slack = jnp.minimum(tallies[source_of] - 1, reach - tallies[sink]) // 2
    slack = jnp.where((source_of == order[0]) | (sink == order[0]) | (tallies[sink] == 0), 0, jnp.maximum(slack, 0))
    shifted = jax.random.randint(jax.random.fold_in(own, 4), (amount // 2,), 0, 1 << 20) % (slack + 1)
    tallies = tallies.at[source_of].add(-shifted).at[sink].add(shifted)
    items = jnp.searchsorted(jnp.cumsum(tallies), jnp.arange(rows * top), side="right").astype(jnp.int32)
    grid = items.reshape(top, rows).T
    grid = grid[jax.random.permutation(jax.random.fold_in(own, 1), rows)]
    rotation = jax.random.randint(jax.random.fold_in(own, 2), (rows, 1), 0, top)
    return jnp.take_along_axis(grid, (jnp.arange(top)[None, :] + rotation) % top, axis=1)


def shares(amount, total, bound, slope, full):
    portions = [(1 << 20) // math.isqrt(standing ** slope) + 1 for standing in range(1, amount + 1)]
    largest = bound if full else min(bound, max(-(-total // amount), total * portions[0] // sum(portions)))
    least = 1 if total - largest >= amount - 1 else 0
    counts, rest = [largest] + [least] * (amount - 1), total - largest - least * (amount - 1)
    while rest > 0:
        candidates = [i for i in range(1, amount) if counts[i] < largest] or [i for i in range(1, amount) if counts[i] < bound]
        mass, left = sum([portions[i] for i in candidates]), rest
        for i in candidates:
            more = min(bound - counts[i], max(1, left * portions[i] // mass), rest)
            counts[i] = counts[i] + more
            rest = rest - more
    return np.array(counts)


def gaussian(key, extent, width, reach, cuts=(), kind=jnp.bfloat16):
    drawn = jax.random.normal(key, extent, jnp.float32) * width
    if len(cuts) > 0:
        drawn = block_levels(key, extent, cuts, -0.22, 0.18) * drawn
    return jnp.clip(drawn, min=-reach, max=reach).astype(kind)


def setup_inputs(seed: int = 0) -> dict:
    arg_keys = jax.random.split(jax.random.key(seed), 5)
    inverse = draw_inverse(jax.random.fold_in(arg_keys[4], 71), 0)
    tiles = gaussian(arg_keys[1], (TILES, 2 * BLOCK), 1.0, 6.0, ((0, 32),))
    tile_dest_keys = jax.random.split(jax.random.fold_in(arg_keys[2], 1), TILES // TPD)
    tile_dest_turns = jax.random.permutation(jax.random.fold_in(arg_keys[2], 3), TILES // TPD)
    tile_dest = jax.vmap(lambda own, number: assign_block(jax.random.fold_in(arg_keys[2], 2), own, number, TPD, N_LAYER * N_LAT, 1, CAP, 2))(tile_dest_keys, tile_dest_turns).reshape((TILES, 1))
    tile_code = touch_ends(jax.random.randint(arg_keys[3], (TILES,), 0, SRC * DEP * NB), jax.random.fold_in(arg_keys[3], 1), 0, (SRC * DEP * NB) - 1).astype(jnp.int32)
    return {"inverse": inverse, "tiles": tiles, "tile_dest": tile_dest, "tile_code": tile_code}


def apply_block(matrix, vectors):
    return jnp.einsum("bij,bsj->bsi", matrix, vectors, precision=lax.Precision.HIGHEST)


def reference(inverse, tiles, tile_dest, tile_code):
    trace_len = 2 * BLOCK
    far_rows = trace_len * (DEP - 1)
    target = tile_dest[:, 0]
    layer_at = target // N_LAT
    block_at = (target % N_LAT) * NB + tile_code % NB
    plane_at = (tile_code // NB) % DEP
    source_at = tile_code // (NB * DEP)
    segment = ((layer_at * BLOCKS + block_at) * SRC + source_at) * DEP + plane_at
    summed = jax.ops.segment_sum(tiles.astype(jnp.float32), segment.astype(jnp.int32), num_segments=N_LAYER * BLOCKS * SRC * DEP)
    source_field = lax.optimization_barrier(summed.reshape(N_LAYER, BLOCKS, SRC, M).astype(jnp.bfloat16))

    def solve_layer(pieces):
        matrix, vectors = pieces
        return apply_block(matrix.astype(jnp.float32), vectors.astype(jnp.float32))

    local_solve = lax.map(solve_layer, (inverse, source_field))
    down_matrix = inverse[:, :, far_rows:, :trace_len].astype(jnp.float32)
    up_matrix = inverse[:, :, :trace_len, far_rows:].astype(jnp.float32)
    empty = jnp.zeros((BLOCKS, SRC, trace_len), jnp.float32)

    def sweep_step(before, pieces):
        matrix, offset = pieces
        after = apply_block(matrix, before) + offset
        return after, before

    _, from_above = lax.scan(sweep_step, empty, (down_matrix, local_solve[:, :, :, far_rows:]))
    _, from_below = lax.scan(sweep_step, empty, (up_matrix, local_solve[:, :, :, :trace_len]), reverse=True)
    above_trace = lax.optimization_barrier(from_above.astype(jnp.bfloat16))
    below_trace = lax.optimization_barrier(from_below.astype(jnp.bfloat16))

    def finish_layer(pieces):
        matrix, local_part, above_part, below_part = pieces
        matrix_wide = matrix.astype(jnp.float32)
        result = local_part + apply_block(matrix_wide[:, :, :trace_len], above_part.astype(jnp.float32))
        return result + apply_block(matrix_wide[:, :, far_rows:], below_part.astype(jnp.float32))

    return lax.map(finish_layer, (inverse, local_solve, above_trace, below_trace))
```

```python
import functools

import jax
import jax.numpy as jnp
from jax import lax
from jax.experimental import pallas as pl
from jax.experimental.pallas import tpu as pltpu
from jax.sharding import PartitionSpec as P

MESH = pl.DeviceIdType.MESH
F32 = jnp.float32
BF16 = jnp.bfloat16
GROUP = 32
QUAD = 4


def nt(vectors, matrix):
    return lax.dot_general(vectors, matrix, (((1,), (1,)), ((), ())), preferred_element_type=F32)


def kernel(
    layers, lateral,
    inv, tiles_in, dest_in, code_in, out,
    tiles, dest, code, send, recv, chalf, ohalf, far, zfar, comp, acc, base, give, po, cin, oin, qin, qout, fout,
    small_sem, load_sem, late, send_sem, recv_sem, far_send, far_recv, zfar_send, zfar_recv,
    po_send, po_recv, t_send, c_send, c_recv, o_send, o_recv, q_send, q_recv,
):
    layer = lax.axis_index("layer")
    lat = lax.axis_index("lat")
    devices = layers * lateral
    me = layer * lateral + lat
    x = lax.rem(layer, 2)
    group = layer // 2
    groups = layers // 2
    step = 2 * x - 1
    place = jnp.where(x == 1, group, groups - 1 - group)
    blocks, size, r = chalf.shape
    count = tiles.shape[0]
    mine = pl.multiple_of((1 - x) * r, r)
    other = pl.multiple_of(x * r, r)
    first = place == 0
    last = place == groups - 1
    odd = lax.rem(place, 2) == 1

    column = 2 * layers
    rank = (lat // 2) * column + layer * 2 + lax.rem(lat, 2)
    quad = rank // QUAD
    quads = devices // QUAD

    def locate(at):
        return lax.rem(at // 2, layers), (at // column) * 2 + lax.rem(at, 2)

    smalls = [
        pltpu.make_async_copy(source, target, small_sem.at[i])
        for i, (source, target) in enumerate(((tiles_in, tiles), (dest_in, dest), (code_in, code)))
    ]
    for load in smalls:
        load.start()
    loads = [
        pltpu.make_async_copy(inv.at[0, :, :, pl.ds(mine, r)], chalf, load_sem.at[0]),
        pltpu.make_async_copy(inv.at[0, :, :, pl.ds(other, r)], ohalf, load_sem.at[1]),
    ]
    for load in loads:
        load.start()

    barrier = pltpu.get_barrier_semaphore()

    @pl.loop(rank + 1, devices)
    def _(at):
        pl.semaphore_signal(barrier, inc=1, device_id=locate(at), device_id_type=MESH)

    @pl.when(rank > 0)
    def _():
        pl.semaphore_wait(barrier, rank)

    @pl.loop(0, rank)
    def _(at):
        pl.semaphore_signal(late.at[quad], inc=1, device_id=locate(at), device_id_type=MESH)

    for load in smalls:
        load.wait()

    row_t = lax.broadcasted_iota(jnp.int32, (count, count), 0)
    col_t = lax.broadcasted_iota(jnp.int32, (count, count), 1)
    target = dest[...]
    across = jnp.broadcast_to(target, (count, count))
    named = jnp.sum(jnp.where(row_t == col_t, across, 0), axis=1, keepdims=True)
    order = jnp.sum(
        jnp.where((named == target) & (row_t < col_t), 1, 0), axis=0, keepdims=True
    )
    codes = jnp.broadcast_to(code[...], (count, count)) + 1
    code_col = jnp.sum(jnp.where(row_t == col_t, codes, 0), axis=1, keepdims=True)
    half = r // 2
    parts = [
        tiles[:, :half],
        tiles[:, half:],
        jnp.broadcast_to(code_col, (count, half)).astype(F32).astype(BF16),
    ]
    shape_w = (GROUP * 8, count)
    row_w = lax.broadcasted_iota(jnp.int32, shape_w, 0)
    q_w = row_w % 8
    slot_w = jnp.where(q_w < 4, q_w // 2, q_w - 4)
    kind_w = jnp.where(q_w < 4, q_w % 2, jnp.where(q_w < 6, 2, 3))

    def pack(chunk):
        hit = (target == chunk * GROUP + row_w // 8) & (order == slot_w)
        message = jnp.zeros((GROUP * 8, half), F32)
        for kind, part in enumerate(parts):
            picks = jnp.where(hit & (kind_w == kind), 1.0, 0.0).astype(BF16)
            message = message + jnp.dot(picks, part, preferred_element_type=F32)
        send[pl.ds(chunk * GROUP, GROUP)] = message.reshape(GROUP, 8, half).astype(BF16)

    if devices == GROUP:
        pack(0)
    else:
        pl.loop(0, devices // GROUP)(pack)
    recv[me] = send[me]

    def route(at):
        to_layer, to_lat = locate(at)
        pltpu.make_async_remote_copy(
            src_ref=send.at[to_layer * lateral + to_lat],
            dst_ref=recv.at[me],
            send_sem=send_sem,
            recv_sem=recv_sem,
            device_id=(to_layer, to_lat),
            device_id_type=MESH,
        ).start()

    def copy(source, target, send_at, recv_at, to):
        return pltpu.make_async_remote_copy(
            src_ref=source, dst_ref=target, send_sem=send_at, recv_sem=recv_at,
            device_id=(to, lat), device_id_type=MESH,
        )

    partner = layer - step
    far_copy = copy(inv.at[0, :, pl.ds(mine, r), pl.ds(other, r)], far, far_send, far_recv, partner)
    raw_copy = copy(
        inv.at[0, :, pl.ds(other, r), pl.ds(mine, r)], zfar, zfar_send, zfar_recv, layer + 2 * step
    )
    comp_copy = copy(comp, zfar, zfar_send, zfar_recv, layer + 2 * step)

    @pl.loop(0, rank)
    def _(i):
        route(rank - 1 - i)

    rest = QUAD - 1 - lax.rem(rank, QUAD)

    @pl.when(rest > 0)
    def _():
        pl.semaphore_wait(late.at[quad], rest)

    @pl.loop(rank + 1, (quad + 1) * QUAD)
    def _(at):
        route(at)

    def route_quad(q):
        pl.semaphore_wait(late.at[q], QUAD)
        for i in range(QUAD):
            route(q * QUAD + i)

    bound = (lat // 2 + 1) * (column // QUAD)
    pl.loop(quad + 1, bound)(route_quad)

    @pl.when(jnp.logical_not(first | last))
    def _():
        far_copy.start()

    pl.loop(bound, quads)(route_quad)

    @pl.when(first)
    def _():
        raw_copy.start()
        far_copy.start()

    for load in loads:
        load.wait()

    everyone = pl.ds(0, devices - 1)
    pltpu.make_async_copy(recv.at[everyone], recv.at[everyone], recv_sem).wait()

    shape_u = (GROUP, 8, half)
    q_u = lax.broadcasted_iota(jnp.int32, shape_u, 1)
    lane = lax.broadcasted_iota(jnp.int32, shape_u, 2)
    s_of, half_of, plane_of, block_of = lane % 8, (lane // 8) % 2, (lane // 16) % 2, lane // 32
    wanted = (((s_of * 2 + plane_of) * blocks + block_of) + 1).astype(F32)
    usable = (q_u < 4) & (q_u % 2 == half_of) & (lane < 64)

    def unpack(chunk):
        got = recv[pl.ds(chunk * GROUP, GROUP)].astype(F32)
        named_code = jnp.where(q_u < 2, got[:, 4:5, :], got[:, 5:6, :])
        table = jnp.where(usable & (named_code == wanted), 1.0, 0.0)
        return lax.dot_general(
            table.reshape(GROUP * 8, half).astype(BF16),
            got.reshape(GROUP * 8, half).astype(BF16),
            (((0,), (0,)), ((), ())),
            preferred_element_type=F32,
        )

    if devices == GROUP:
        field = unpack(0)
    else:
        field = lax.fori_loop(
            0, devices // GROUP, lambda i, total: total + unpack(i), jnp.zeros((half, half), F32)
        )

    upper = x == 1
    for b in range(blocks):
        rows = [field[32 * b + 8 * k : 32 * b + 8 * k + 8] for k in range(4)]
        top = jnp.concatenate(rows[:2], axis=1)
        bottom = jnp.concatenate(rows[2:], axis=1)
        own = jnp.where(upper, top, bottom).astype(BF16)
        away = jnp.where(upper, bottom, top).astype(BF16)
        local = nt(own, chalf[b]) + nt(away, ohalf[b])
        acc[b] = local
        give[b] = jnp.where(upper, local[:, :r], local[:, r:]).astype(BF16)
        owned = jnp.where(upper, local[:, r:], local[:, :r])
        base[b] = owned
        qout[b] = owned.astype(BF16)

    def step_of(b):
        return chalf[b, pl.ds(other, r), :]

    po_copy = copy(give, po, po_send, po_recv, partner)
    start_copy = copy(give, cin, t_send, c_recv, layer - 3 * step)
    q_copy = copy(qout, qin, q_send, q_recv, layer + 2 * step)
    c_copies = [
        copy(fout, cin, c_send.at[i], c_recv, layer + (2 + 2 * i) * step) for i in range(2)
    ]
    o_copy = copy(fout, oin, o_send, o_recv, layer + step)

    @pl.when(last)
    def _():
        start_copy.start()

    po_copy.start()

    @pl.when(first)
    def _():
        q_copy.start()

    def opposite():
        o_copy.wait_recv()
        for b in range(blocks):
            acc[b] = acc[b] + nt(oin[b], ohalf[b])

    @pl.when(first)
    def _():
        po_copy.wait_recv()
        for b in range(blocks):
            fout[b] = (nt(po[b], step_of(b)) + base[b]).astype(BF16)
        o_copy.start()
        for b in range(blocks):
            acc[b] = acc[b] + nt(po[b], chalf[b])
        opposite()

    @pl.when(jnp.logical_not(odd | first))
    def _():
        far_copy.wait_recv()
        for b in range(blocks):
            comp[b] = jnp.dot(step_of(b), far[b], preferred_element_type=F32).astype(BF16)
        comp_copy.start()
        po_copy.wait_recv()
        for b in range(blocks):
            total = nt(po[b], step_of(b)) + base[b]
            base[b] = total
            qout[b] = total.astype(BF16)
        q_copy.start()

        def chain():
            c_copies[0].wait_recv()
            for b in range(blocks):
                fout[b] = (nt(cin[b], comp[b]) + base[b]).astype(BF16)
            o_copy.start()
            for b in range(blocks):
                trace = nt(cin[b], far[b]) + po[b].astype(F32)
                acc[b] = acc[b] + nt(trace.astype(BF16), chalf[b])

        early = 2 * place < groups

        @pl.when(early)
        def _():
            chain()
            opposite()

        @pl.when(jnp.logical_not(early))
        def _():
            opposite()
            chain()

    @pl.when(odd)
    def _():
        far_copy.wait_recv()
        po_copy.wait_recv()
        comp_copy.wait_recv()
        q_copy.wait_recv()
        c_copies[0].wait_recv()
        traces = []
        for b in range(blocks):
            middle = nt(cin[b], zfar[b]) + qin[b].astype(F32)
            traces.append((nt(middle.astype(BF16), far[b]) + po[b].astype(F32)).astype(BF16))

        @pl.when(jnp.logical_not(last))
        def _():
            for b in range(blocks):
                fout[b] = (nt(traces[b], step_of(b)) + base[b]).astype(BF16)
            c_copies[1].start()
            c_copies[0].start()
            o_copy.start()

        for b in range(blocks):
            acc[b] = acc[b] + nt(traces[b], chalf[b])

        @pl.when(jnp.logical_not(last))
        def _():
            opposite()

    for b in range(blocks):
        out[0, b] = acc[b]

    @pl.when(jnp.logical_not(last))
    def _():
        far_copy.wait_send()
        o_copy.wait_send()

    @pl.when(last)
    def _():
        start_copy.wait_send()

    @pl.when(jnp.logical_not(odd))
    def _():
        comp_copy.wait_send()
        q_copy.wait_send()

    @pl.when(odd & jnp.logical_not(last))
    def _():
        for c_copy in c_copies:
            c_copy.wait_send()

    po_copy.wait_send()
    pltpu.make_async_copy(send.at[everyone], send.at[everyone], send_sem).wait()


def body(layers, lateral, inverse, tiles, tile_dest, tile_code):
    devices = layers * lateral
    _, blocks, size, _ = inverse.shape
    r = tiles.shape[1]
    src = 8
    dma = pltpu.SemaphoreType.DMA
    small = (blocks, src, r)
    matrix = pltpu.VMEM((blocks, r, r), BF16)
    vmem = pl.BlockSpec(memory_space=pltpu.VMEM)
    return pl.pallas_call(
        functools.partial(kernel, layers, lateral),
        out_shape=jax.ShapeDtypeStruct((1, blocks, src, size), F32),
        in_specs=[pl.BlockSpec(memory_space=pltpu.HBM)] * 4,
        out_specs=vmem,
        scratch_shapes=[
            pltpu.VMEM(tiles.shape, BF16),
            pltpu.VMEM((1, tiles.shape[0]), jnp.int32),
            pltpu.VMEM((1, tiles.shape[0]), jnp.int32),
            pltpu.VMEM((devices, 8, r // 2), BF16),
            pltpu.VMEM((devices, 8, r // 2), BF16),
            pltpu.VMEM((blocks, size, r), BF16),
            pltpu.VMEM((blocks, size, r), BF16),
            matrix, matrix, matrix,
            pltpu.VMEM((blocks, src, size), F32),
            pltpu.VMEM(small, F32),
        ]
        + [pltpu.VMEM(small, BF16)] * 7
        + [dma((3,)), dma((2,)), pltpu.SemaphoreType.REGULAR((devices // QUAD,))]
        + [dma] * 9
        + [dma((2,))]
        + [dma] * 5,
        compiler_params=pltpu.CompilerParams(
            collective_id=0, has_side_effects=True, vmem_limit_bytes=48 * 1024 * 1024
        ),
        name="sweep",
    )(
        *(
            pltpu.with_memory_space_constraint(array, pltpu.HBM)
            for array in (inverse, tiles, tile_dest.reshape(1, -1), tile_code.reshape(1, -1))
        )
    )


def solution(mesh):
    in_specs = (
        P("layer", "lat", None, None),
        P(("layer", "lat"), None),
        P(("layer", "lat"), None),
        P(("layer", "lat")),
    )
    out_specs = P("layer", "lat", None, None)
    return jax.shard_map(
        functools.partial(body, mesh.shape["layer"], mesh.shape["lat"]),
        mesh=mesh, in_specs=in_specs, out_specs=out_specs, check_vma=False,
    )
```

```python
import functools

import jax
import jax.numpy as jnp
from jax import lax
from jax.experimental import pallas as pl
from jax.experimental.pallas import tpu as pltpu
from jax.sharding import PartitionSpec as P

MESH = pl.DeviceIdType.MESH
F32 = jnp.float32
BF16 = jnp.bfloat16
GROUP = 32


def nt(vectors, matrix):
    return lax.dot_general(vectors, matrix, (((1,), (1,)), ((), ())), preferred_element_type=F32)


def kernel(
    layers, lateral,
    inv, tiles_in, dest_in, code_in, out,
    tiles, dest, code, send, recv, chalf, ohalf, far, zfar, comp, acc, base, give, po, cin, oin, qin, qout, fout,
    small_sem, load_sem, send_sem, recv_sem, far_send, far_recv, zfar_send, zfar_recv,
    po_send, po_recv, t_send, c_send, c_recv, o_send, o_recv, q_send, q_recv,
):
    layer = lax.axis_index("layer")
    lat = lax.axis_index("lat")
    devices = layers * lateral
    me = layer * lateral + lat
    x = lax.rem(layer, 2)
    group = layer // 2
    groups = layers // 2
    step = 2 * x - 1
    place = jnp.where(x == 1, group, groups - 1 - group)
    blocks, size, r = chalf.shape
    count = tiles.shape[0]
    mine = pl.multiple_of((1 - x) * r, r)
    other = pl.multiple_of(x * r, r)
    first = place == 0
    last = place == groups - 1
    odd = lax.rem(place, 2) == 1

    def others(visit):
        def visit_layer(i):
            to = layers - 1 - i

            for across in range(1, lateral):
                visit(to, wrap(lat + across, lateral))

            @pl.when(to != layer)
            def _():
                visit(to, lat)

        if devices == GROUP:
            for i in range(layers):
                visit_layer(i)
        else:
            pl.loop(0, layers)(visit_layer)

    def wrap(index, length):
        return jnp.where(index >= length, index - length, index)

    smalls = [
        pltpu.make_async_copy(source, target, small_sem.at[i])
        for i, (source, target) in enumerate(((tiles_in, tiles), (dest_in, dest), (code_in, code)))
    ]
    for load in smalls:
        load.start()
    loads = [
        pltpu.make_async_copy(inv.at[0, :, :, pl.ds(mine, r)], chalf, load_sem.at[0]),
        pltpu.make_async_copy(inv.at[0, :, :, pl.ds(other, r)], ohalf, load_sem.at[1]),
    ]
    for load in loads:
        load.start()

    barrier = pltpu.get_barrier_semaphore()

    def greet(to_layer, to_lat):
        pl.semaphore_signal(
            barrier, inc=1, device_id=(to_layer, to_lat), device_id_type=MESH
        )

    others(greet)

    for load in smalls:
        load.wait()

    row_t = lax.broadcasted_iota(jnp.int32, (count, count), 0)
    col_t = lax.broadcasted_iota(jnp.int32, (count, count), 1)
    target = dest[...]
    across = jnp.broadcast_to(target, (count, count))
    named = jnp.sum(jnp.where(row_t == col_t, across, 0), axis=1, keepdims=True)
    order = jnp.sum(
        jnp.where((named == target) & (row_t < col_t), 1, 0), axis=0, keepdims=True
    )
    codes = jnp.broadcast_to(code[...], (count, count)) + 1
    code_col = jnp.sum(jnp.where(row_t == col_t, codes, 0), axis=1, keepdims=True)
    half = r // 2
    parts = [
        tiles[:, :half],
        tiles[:, half:],
        jnp.broadcast_to(code_col, (count, half)).astype(F32).astype(BF16),
    ]
    shape_w = (GROUP * 8, count)
    row_w = lax.broadcasted_iota(jnp.int32, shape_w, 0)
    q_w = row_w % 8
    slot_w = jnp.where(q_w < 4, q_w // 2, q_w - 4)
    kind_w = jnp.where(q_w < 4, q_w % 2, jnp.where(q_w < 6, 2, 3))

    def pack(chunk):
        hit = (target == chunk * GROUP + row_w // 8) & (order == slot_w)
        message = jnp.zeros((GROUP * 8, half), F32)
        for kind, part in enumerate(parts):
            picks = jnp.where(hit & (kind_w == kind), 1.0, 0.0).astype(BF16)
            message = message + jnp.dot(picks, part, preferred_element_type=F32)
        send[pl.ds(chunk * GROUP, GROUP)] = message.reshape(GROUP, 8, half).astype(BF16)

    if devices == GROUP:
        pack(0)
    else:
        pl.loop(0, devices // GROUP)(pack)
    recv[me] = send[me]

    pl.semaphore_wait(barrier, devices - 1)

    def route(to_layer, to_lat):
        pltpu.make_async_remote_copy(
            src_ref=send.at[to_layer * lateral + to_lat],
            dst_ref=recv.at[me],
            send_sem=send_sem,
            recv_sem=recv_sem,
            device_id=(to_layer, to_lat),
            device_id_type=MESH,
        ).start()

    def copy(source, target, send_at, recv_at, to):
        return pltpu.make_async_remote_copy(
            src_ref=source, dst_ref=target, send_sem=send_at, recv_sem=recv_at,
            device_id=(to, lat), device_id_type=MESH,
        )

    partner = layer - step
    onward = layer + 2 * step
    far_copies = [
        copy(
            inv.at[0, b, pl.ds(mine, r), pl.ds(other, r)], far.at[b],
            far_send.at[b], far_recv.at[b], partner,
        )
        for b in range(blocks)
    ]
    raw_copies = [
        copy(
            inv.at[0, b, pl.ds(other, r), pl.ds(mine, r)], zfar.at[b],
            zfar_send.at[b], zfar_recv.at[b], onward,
        )
        for b in range(blocks)
    ]
    comp_copies = [
        copy(comp.at[b], zfar.at[b], zfar_send.at[b], zfar_recv.at[b], onward)
        for b in range(blocks)
    ]

    others(route)

    @pl.when(first)
    def _():
        for raw_copy in raw_copies:
            raw_copy.start()

    @pl.when(jnp.logical_not(last))
    def _():
        for far_copy in far_copies:
            far_copy.start()

    for load in loads:
        load.wait()

    everyone = pl.ds(0, devices - 1)
    pltpu.make_async_copy(recv.at[everyone], recv.at[everyone], recv_sem).wait()

    shape_u = (GROUP, 8, half)
    q_u = lax.broadcasted_iota(jnp.int32, shape_u, 1)
    lane = lax.broadcasted_iota(jnp.int32, shape_u, 2)
    s_of, half_of, plane_of, block_of = lane % 8, (lane // 8) % 2, (lane // 16) % 2, lane // 32
    wanted = (((s_of * 2 + plane_of) * blocks + block_of) + 1).astype(F32)
    usable = (q_u < 4) & (q_u % 2 == half_of) & (lane < 64)

    def unpack(chunk):
        got = recv[pl.ds(chunk * GROUP, GROUP)].astype(F32)
        named_code = jnp.where(q_u < 2, got[:, 4:5, :], got[:, 5:6, :])
        table = jnp.where(usable & (named_code == wanted), 1.0, 0.0)
        return lax.dot_general(
            table.reshape(GROUP * 8, half).astype(BF16),
            got.reshape(GROUP * 8, half).astype(BF16),
            (((0,), (0,)), ((), ())),
            preferred_element_type=F32,
        )

    if devices == GROUP:
        field = unpack(0)
    else:
        field = lax.fori_loop(
            0, devices // GROUP, lambda i, total: total + unpack(i), jnp.zeros((half, half), F32)
        )

    upper = x == 1
    for b in range(blocks):
        rows = [field[32 * b + 8 * k : 32 * b + 8 * k + 8] for k in range(4)]
        top = jnp.concatenate(rows[:2], axis=1)
        bottom = jnp.concatenate(rows[2:], axis=1)
        own = jnp.where(upper, top, bottom).astype(BF16)
        away = jnp.where(upper, bottom, top).astype(BF16)
        local = nt(own, chalf[b]) + nt(away, ohalf[b])
        acc[b] = local
        give[b] = jnp.where(upper, local[:, :r], local[:, r:]).astype(BF16)
        owned = jnp.where(upper, local[:, r:], local[:, :r])
        base[b] = owned
        qout[b] = owned.astype(BF16)

    def step_of(b):
        return chalf[b, pl.ds(other, r), :]

    po_copy = copy(give, po, po_send, po_recv, partner)
    start_copy = copy(give, cin, t_send, c_recv, layer - 3 * step)
    q_copy = copy(qout, qin, q_send, q_recv, onward)
    c_copies = [
        copy(fout, cin, c_send.at[i], c_recv, layer + (2 + 2 * i) * step) for i in range(2)
    ]
    o_copy = copy(fout, oin, o_send, o_recv, layer + step)

    @pl.when(last)
    def _():
        start_copy.start()

    po_copy.start()

    @pl.when(first)
    def _():
        q_copy.start()

    def opposite():
        o_copy.wait_recv()
        for b in range(blocks):
            acc[b] = acc[b] + nt(oin[b], ohalf[b])

    @pl.when(first)
    def _():
        po_copy.wait_recv()
        for b in range(blocks):
            fout[b] = (nt(po[b], step_of(b)) + base[b]).astype(BF16)
        o_copy.start()
        for b in range(blocks):
            acc[b] = acc[b] + nt(po[b], chalf[b])
        opposite()

    @pl.when(jnp.logical_not(odd | first))
    def _():
        for b in range(blocks):
            far_copies[b].wait_recv()
            comp[b] = jnp.dot(step_of(b), far[b], preferred_element_type=F32).astype(BF16)
            comp_copies[b].start()
        po_copy.wait_recv()
        for b in range(blocks):
            total = nt(po[b], step_of(b)) + base[b]
            base[b] = total
            qout[b] = total.astype(BF16)
        q_copy.start()

        def chain():
            c_copies[0].wait_recv()
            for b in range(blocks):
                fout[b] = (nt(cin[b], comp[b]) + base[b]).astype(BF16)
            o_copy.start()
            for b in range(blocks):
                trace = nt(cin[b], far[b]) + po[b].astype(F32)
                acc[b] = acc[b] + nt(trace.astype(BF16), chalf[b])

        early = 2 * place < groups

        @pl.when(early)
        def _():
            chain()
            opposite()

        @pl.when(jnp.logical_not(early))
        def _():
            opposite()
            chain()

    @pl.when(odd)
    def _():
        for b in range(blocks):
            far_copies[b].wait_recv()
            comp_copies[b].wait_recv()
        po_copy.wait_recv()
        q_copy.wait_recv()
        c_copies[0].wait_recv()
        traces = []
        for b in range(blocks):
            middle = nt(cin[b], zfar[b]) + qin[b].astype(F32)
            traces.append((nt(middle.astype(BF16), far[b]) + po[b].astype(F32)).astype(BF16))

        @pl.when(jnp.logical_not(last))
        def _():
            for b in range(blocks):
                fout[b] = (nt(traces[b], step_of(b)) + base[b]).astype(BF16)
            c_copies[1].start()
            c_copies[0].start()
            o_copy.start()

        for b in range(blocks):
            acc[b] = acc[b] + nt(traces[b], chalf[b])

        @pl.when(jnp.logical_not(last))
        def _():
            opposite()

    for b in range(blocks):
        out[0, b] = acc[b]

    @pl.when(jnp.logical_not(last))
    def _():
        for far_copy in far_copies:
            far_copy.wait_send()
        o_copy.wait_send()

    @pl.when(last)
    def _():
        start_copy.wait_send()

    @pl.when(jnp.logical_not(odd))
    def _():
        for comp_copy in comp_copies:
            comp_copy.wait_send()
        q_copy.wait_send()

    @pl.when(odd & jnp.logical_not(last))
    def _():
        for c_copy in c_copies:
            c_copy.wait_send()

    po_copy.wait_send()
    pltpu.make_async_copy(send.at[everyone], send.at[everyone], send_sem).wait()


def body(layers, lateral, inverse, tiles, tile_dest, tile_code):
    devices = layers * lateral
    _, blocks, size, _ = inverse.shape
    r = tiles.shape[1]
    src = 8
    dma = pltpu.SemaphoreType.DMA
    small = (blocks, src, r)
    matrix = pltpu.VMEM((blocks, r, r), BF16)
    vmem = pl.BlockSpec(memory_space=pltpu.VMEM)
    return pl.pallas_call(
        functools.partial(kernel, layers, lateral),
        out_shape=jax.ShapeDtypeStruct((1, blocks, src, size), F32),
        in_specs=[pl.BlockSpec(memory_space=pltpu.HBM)] * 4,
        out_specs=vmem,
        scratch_shapes=[
            pltpu.VMEM(tiles.shape, BF16),
            pltpu.VMEM((1, tiles.shape[0]), jnp.int32),
            pltpu.VMEM((1, tiles.shape[0]), jnp.int32),
            pltpu.VMEM((devices, 8, r // 2), BF16),
            pltpu.VMEM((devices, 8, r // 2), BF16),
            pltpu.VMEM((blocks, size, r), BF16),
            pltpu.VMEM((blocks, size, r), BF16),
            matrix, matrix, matrix,
            pltpu.VMEM((blocks, src, size), F32),
            pltpu.VMEM(small, F32),
        ]
        + [pltpu.VMEM(small, BF16)] * 7
        + [dma((3,)), dma((2,)), dma, dma]
        + [dma((blocks,))] * 4
        + [dma] * 3
        + [dma((2,))]
        + [dma] * 5,
        compiler_params=pltpu.CompilerParams(
            collective_id=0, has_side_effects=True, vmem_limit_bytes=48 * 1024 * 1024
        ),
        name="sweep",
    )(
        *(
            pltpu.with_memory_space_constraint(array, pltpu.HBM)
            for array in (inverse, tiles, tile_dest.reshape(1, -1), tile_code.reshape(1, -1))
        )
    )


def solution(mesh):
    in_specs = (
        P("layer", "lat", None, None),
        P(("layer", "lat"), None),
        P(("layer", "lat"), None),
        P(("layer", "lat")),
    )
    out_specs = P("layer", "lat", None, None)
    return jax.shard_map(
        functools.partial(body, mesh.shape["layer"], mesh.shape["lat"]),
        mesh=mesh, in_specs=in_specs, out_specs=out_specs, check_vma=False,
    )
```

```python
import functools

import jax
import jax.numpy as jnp
from jax import lax
from jax.experimental import pallas as pl
from jax.experimental.pallas import tpu as pltpu
from jax.sharding import PartitionSpec as P

MESH = pl.DeviceIdType.MESH
F32 = jnp.float32
BF16 = jnp.bfloat16
GROUP = 32


def nt(vectors, matrix):
    return lax.dot_general(vectors, matrix, (((1,), (1,)), ((), ())), preferred_element_type=F32)


def kernel(
    layers, lateral,
    inv, tiles_in, dest_in, code_in, out,
    tiles, dest, code, send, recv, chalf, ohalf, far, zfar, comp, acc, base, give, po, cin, oin, qin, qout, fout,
    small_sem, load_sem, send_sem, recv_sem, far_send, far_recv, zfar_send, zfar_recv,
    po_send, po_recv, t_send, c_send, c_recv, o_send, o_recv, q_send, q_recv,
):
    layer = lax.axis_index("layer")
    lat = lax.axis_index("lat")
    devices = layers * lateral
    me = layer * lateral + lat
    x = lax.rem(layer, 2)
    group = layer // 2
    groups = layers // 2
    step = 2 * x - 1
    place = jnp.where(x == 1, group, groups - 1 - group)
    blocks, size, r = chalf.shape
    count = tiles.shape[0]
    mine = pl.multiple_of((1 - x) * r, r)
    other = pl.multiple_of(x * r, r)
    first = place == 0
    last = place == groups - 1
    odd = lax.rem(place, 2) == 1

    def others(visit, downward):
        def visit_layer(i):
            to = layers - 1 - i if downward else i

            for across in range(1, lateral):
                visit(to, wrap(lat + across, lateral))

            @pl.when(to != layer)
            def _():
                visit(to, lat)

        if devices == GROUP:
            for i in range(layers):
                visit_layer(i)
        else:
            pl.loop(0, layers)(visit_layer)

    def wrap(index, length):
        return jnp.where(index >= length, index - length, index)

    smalls = [
        pltpu.make_async_copy(source, target, small_sem.at[i])
        for i, (source, target) in enumerate(((tiles_in, tiles), (dest_in, dest), (code_in, code)))
    ]
    for load in smalls:
        load.start()
    loads = [
        pltpu.make_async_copy(inv.at[0, :, :, pl.ds(mine, r)], chalf, load_sem.at[0]),
        pltpu.make_async_copy(inv.at[0, :, :, pl.ds(other, r)], ohalf, load_sem.at[1]),
    ]
    for load in loads:
        load.start()

    barrier = pltpu.get_barrier_semaphore()

    def greet(to_layer, to_lat):
        pl.semaphore_signal(
            barrier, inc=1, device_id=(to_layer, to_lat), device_id_type=MESH
        )

    others(greet, False)

    for load in smalls:
        load.wait()

    row_t = lax.broadcasted_iota(jnp.int32, (count, count), 0)
    col_t = lax.broadcasted_iota(jnp.int32, (count, count), 1)
    target = dest[...]
    across = jnp.broadcast_to(target, (count, count))
    named = jnp.sum(jnp.where(row_t == col_t, across, 0), axis=1, keepdims=True)
    order = jnp.sum(
        jnp.where((named == target) & (row_t < col_t), 1, 0), axis=0, keepdims=True
    )
    codes = jnp.broadcast_to(code[...], (count, count)) + 1
    code_col = jnp.sum(jnp.where(row_t == col_t, codes, 0), axis=1, keepdims=True)
    half = r // 2
    parts = [
        tiles[:, :half],
        tiles[:, half:],
        jnp.broadcast_to(code_col, (count, half)).astype(F32).astype(BF16),
    ]
    shape_w = (GROUP * 8, count)
    row_w = lax.broadcasted_iota(jnp.int32, shape_w, 0)
    q_w = row_w % 8
    slot_w = jnp.where(q_w < 4, q_w // 2, q_w - 4)
    kind_w = jnp.where(q_w < 4, q_w % 2, jnp.where(q_w < 6, 2, 3))

    def pack(chunk):
        hit = (target == chunk * GROUP + row_w // 8) & (order == slot_w)
        message = jnp.zeros((GROUP * 8, half), F32)
        for kind, part in enumerate(parts):
            picks = jnp.where(hit & (kind_w == kind), 1.0, 0.0).astype(BF16)
            message = message + jnp.dot(picks, part, preferred_element_type=F32)
        send[pl.ds(chunk * GROUP, GROUP)] = message.reshape(GROUP, 8, half).astype(BF16)

    if devices == GROUP:
        pack(0)
    else:
        pl.loop(0, devices // GROUP)(pack)
    recv[me] = send[me]

    pl.semaphore_wait(barrier, devices - 1)

    def route(to_layer, to_lat):
        pltpu.make_async_remote_copy(
            src_ref=send.at[to_layer * lateral + to_lat],
            dst_ref=recv.at[me],
            send_sem=send_sem,
            recv_sem=recv_sem,
            device_id=(to_layer, to_lat),
            device_id_type=MESH,
        ).start()

    def copy(source, target, send_at, recv_at, to):
        return pltpu.make_async_remote_copy(
            src_ref=source, dst_ref=target, send_sem=send_at, recv_sem=recv_at,
            device_id=(to, lat), device_id_type=MESH,
        )

    partner = layer - step
    onward = layer + 2 * step
    parts_of = [(b, pl.ds(h, half)) for b in range(blocks) for h in range(0, r, half)]
    far_copies = [
        copy(
            inv.at[0, b, pl.ds(mine, r), pl.ds(pl.multiple_of(other + h.start, half), half)],
            far.at[b, :, h], far_send.at[i], far_recv.at[i], partner,
        )
        for i, (b, h) in enumerate(parts_of)
    ]
    raw_copies = [
        copy(
            inv.at[0, b, pl.ds(other, r), pl.ds(pl.multiple_of(mine + h.start, half), half)],
            zfar.at[b, :, h], zfar_send.at[i], zfar_recv.at[i], onward,
        )
        for i, (b, h) in enumerate(parts_of)
    ]
    comp_copies = [
        copy(comp.at[b, :, h], zfar.at[b, :, h], zfar_send.at[i], zfar_recv.at[i], onward)
        for i, (b, h) in enumerate(parts_of)
    ]

    for across in range(lateral):
        route(partner, wrap(lat + across, lateral))

    @pl.when(jnp.logical_not(first | last))
    def _():
        for far_copy in far_copies:
            far_copy.start()

    def route_far(to_layer, to_lat):
        @pl.when(to_layer != partner)
        def _():
            route(to_layer, to_lat)

    others(route_far, True)

    @pl.when(first)
    def _():
        for raw_copy in raw_copies:
            raw_copy.start()

    @pl.when(first)
    def _():
        for far_copy in far_copies:
            far_copy.start()

    for load in loads:
        load.wait()

    def step_of(b):
        return chalf[b, pl.ds(other, r), :]

    def compose(i):
        b, h = parts_of[i]
        far_copies[i].wait_recv()
        comp[b, :, h] = jnp.dot(
            step_of(b), far[b, :, h], preferred_element_type=F32
        ).astype(BF16)
        comp_copies[i].start()

    middle = jnp.logical_not(odd | first)

    @pl.when(middle & (x == 0))
    def _():
        for i in range(2):
            compose(i)

    everyone = pl.ds(0, devices - 1)
    pltpu.make_async_copy(recv.at[everyone], recv.at[everyone], recv_sem).wait()

    shape_u = (GROUP, 8, half)
    q_u = lax.broadcasted_iota(jnp.int32, shape_u, 1)
    lane = lax.broadcasted_iota(jnp.int32, shape_u, 2)
    s_of, half_of, plane_of, block_of = lane % 8, (lane // 8) % 2, (lane // 16) % 2, lane // 32
    wanted = (((s_of * 2 + plane_of) * blocks + block_of) + 1).astype(F32)
    usable = (q_u < 4) & (q_u % 2 == half_of) & (lane < 64)

    def unpack(chunk):
        got = recv[pl.ds(chunk * GROUP, GROUP)].astype(F32)
        named_code = jnp.where(q_u < 2, got[:, 4:5, :], got[:, 5:6, :])
        table = jnp.where(usable & (named_code == wanted), 1.0, 0.0)
        return lax.dot_general(
            table.reshape(GROUP * 8, half).astype(BF16),
            got.reshape(GROUP * 8, half).astype(BF16),
            (((0,), (0,)), ((), ())),
            preferred_element_type=F32,
        )

    if devices == GROUP:
        field = unpack(0)
    else:
        field = lax.fori_loop(
            0, devices // GROUP, lambda i, total: total + unpack(i), jnp.zeros((half, half), F32)
        )

    upper = x == 1
    for b in range(blocks):
        rows = [field[32 * b + 8 * k : 32 * b + 8 * k + 8] for k in range(4)]
        top = jnp.concatenate(rows[:2], axis=1)
        bottom = jnp.concatenate(rows[2:], axis=1)
        own = jnp.where(upper, top, bottom).astype(BF16)
        away = jnp.where(upper, bottom, top).astype(BF16)
        local = nt(own, chalf[b]) + nt(away, ohalf[b])
        acc[b] = local
        give[b] = jnp.where(upper, local[:, :r], local[:, r:]).astype(BF16)
        owned = jnp.where(upper, local[:, r:], local[:, :r])
        base[b] = owned
        qout[b] = owned.astype(BF16)

    po_copy = copy(give, po, po_send, po_recv, partner)
    start_copy = copy(give, cin, t_send, c_recv, layer - 3 * step)
    q_copy = copy(qout, qin, q_send, q_recv, onward)
    c_copies = [
        copy(fout, cin, c_send.at[i], c_recv, layer + (2 + 2 * i) * step) for i in range(2)
    ]
    o_copy = copy(fout, oin, o_send, o_recv, layer + step)

    @pl.when(last)
    def _():
        start_copy.start()

    po_copy.start()

    @pl.when(first)
    def _():
        q_copy.start()

    def opposite():
        o_copy.wait_recv()
        for b in range(blocks):
            acc[b] = acc[b] + nt(oin[b], ohalf[b])

    @pl.when(first)
    def _():
        po_copy.wait_recv()
        for b in range(blocks):
            fout[b] = (nt(po[b], step_of(b)) + base[b]).astype(BF16)
        o_copy.start()
        for b in range(blocks):
            acc[b] = acc[b] + nt(po[b], chalf[b])
        opposite()

    @pl.when(middle)
    def _():
        @pl.when(x == 1)
        def _():
            for i in range(2):
                compose(i)

        for i in range(2, len(parts_of)):
            compose(i)
        po_copy.wait_recv()
        for b in range(blocks):
            total = nt(po[b], step_of(b)) + base[b]
            base[b] = total
            qout[b] = total.astype(BF16)
        q_copy.start()

        def chain():
            c_copies[0].wait_recv()
            for b in range(blocks):
                fout[b] = (nt(cin[b], comp[b]) + base[b]).astype(BF16)
            o_copy.start()
            for b in range(blocks):
                trace = nt(cin[b], far[b]) + po[b].astype(F32)
                acc[b] = acc[b] + nt(trace.astype(BF16), chalf[b])

        early = 2 * place < groups

        @pl.when(early)
        def _():
            chain()
            opposite()

        @pl.when(jnp.logical_not(early))
        def _():
            opposite()
            chain()

    @pl.when(odd)
    def _():
        for i in range(len(parts_of)):
            far_copies[i].wait_recv()
            comp_copies[i].wait_recv()
        po_copy.wait_recv()
        q_copy.wait_recv()
        c_copies[0].wait_recv()
        traces = []
        for b in range(blocks):
            between = nt(cin[b], zfar[b]) + qin[b].astype(F32)
            traces.append((nt(between.astype(BF16), far[b]) + po[b].astype(F32)).astype(BF16))

        @pl.when(jnp.logical_not(last))
        def _():
            for b in range(blocks):
                fout[b] = (nt(traces[b], step_of(b)) + base[b]).astype(BF16)
            c_copies[1].start()
            c_copies[0].start()
            o_copy.start()

        for b in range(blocks):
            acc[b] = acc[b] + nt(traces[b], chalf[b])

        @pl.when(jnp.logical_not(last))
        def _():
            opposite()

    for b in range(blocks):
        out[0, b] = acc[b]

    @pl.when(jnp.logical_not(last))
    def _():
        for far_copy in far_copies:
            far_copy.wait_send()
        o_copy.wait_send()

    @pl.when(last)
    def _():
        start_copy.wait_send()

    @pl.when(jnp.logical_not(odd))
    def _():
        for comp_copy in comp_copies:
            comp_copy.wait_send()
        q_copy.wait_send()

    @pl.when(odd & jnp.logical_not(last))
    def _():
        for c_copy in c_copies:
            c_copy.wait_send()

    po_copy.wait_send()
    pltpu.make_async_copy(send.at[everyone], send.at[everyone], send_sem).wait()


def body(layers, lateral, inverse, tiles, tile_dest, tile_code):
    devices = layers * lateral
    _, blocks, size, _ = inverse.shape
    r = tiles.shape[1]
    src = 8
    dma = pltpu.SemaphoreType.DMA
    small = (blocks, src, r)
    matrix = pltpu.VMEM((blocks, r, r), BF16)
    vmem = pl.BlockSpec(memory_space=pltpu.VMEM)
    return pl.pallas_call(
        functools.partial(kernel, layers, lateral),
        out_shape=jax.ShapeDtypeStruct((1, blocks, src, size), F32),
        in_specs=[pl.BlockSpec(memory_space=pltpu.HBM)] * 4,
        out_specs=vmem,
        scratch_shapes=[
            pltpu.VMEM(tiles.shape, BF16),
            pltpu.VMEM((1, tiles.shape[0]), jnp.int32),
            pltpu.VMEM((1, tiles.shape[0]), jnp.int32),
            pltpu.VMEM((devices, 8, r // 2), BF16),
            pltpu.VMEM((devices, 8, r // 2), BF16),
            pltpu.VMEM((blocks, size, r), BF16),
            pltpu.VMEM((blocks, size, r), BF16),
            matrix, matrix, matrix,
            pltpu.VMEM((blocks, src, size), F32),
            pltpu.VMEM(small, F32),
        ]
        + [pltpu.VMEM(small, BF16)] * 7
        + [dma((3,)), dma((2,)), dma, dma]
        + [dma((2 * blocks,))] * 4
        + [dma] * 3
        + [dma((2,))]
        + [dma] * 5,
        compiler_params=pltpu.CompilerParams(
            collective_id=0, has_side_effects=True, vmem_limit_bytes=48 * 1024 * 1024
        ),
        name="sweep",
    )(
        *(
            pltpu.with_memory_space_constraint(array, pltpu.HBM)
            for array in (inverse, tiles, tile_dest.reshape(1, -1), tile_code.reshape(1, -1))
        )
    )


def solution(mesh):
    in_specs = (
        P("layer", "lat", None, None),
        P(("layer", "lat"), None),
        P(("layer", "lat"), None),
        P(("layer", "lat")),
    )
    out_specs = P("layer", "lat", None, None)
    return jax.shard_map(
        functools.partial(body, mesh.shape["layer"], mesh.shape["lat"]),
        mesh=mesh, in_specs=in_specs, out_specs=out_specs, check_vma=False,
    )
```

```python
import functools

import jax
import jax.numpy as jnp
from jax import lax
from jax.experimental import pallas as pl
from jax.experimental.pallas import tpu as pltpu
from jax.sharding import PartitionSpec as P

MESH = pl.DeviceIdType.MESH
F32 = jnp.float32
BF16 = jnp.bfloat16
GROUP = 32


def nt(vectors, matrix):
    return lax.dot_general(vectors, matrix, (((1,), (1,)), ((), ())), preferred_element_type=F32)


def kernel(
    layers, lateral,
    inv, tiles_in, dest_in, code_in, out,
    tiles, dest, code, send, recv, chalf, ohalf, far, zfar, comp, acc, base, give, po, cin, oin, qin, qout, fout, usib, osib, tout, tin, head, tail,
    small_sem, load_sem, send_sem, recv_sem, far_send, far_recv, zfar_send, zfar_recv,
    po_send, po_recv, t_send, c_send, c_recv, o_send, o_recv, q_send, q_recv,
    head_send, head_recv, tail_send, tail_recv, u_send, u_recv, own_send, own_recv, trace_send, trace_recv,
):
    layer = lax.axis_index("layer")
    lat = lax.axis_index("lat")
    devices = layers * lateral
    me = layer * lateral + lat
    x = lax.rem(layer, 2)
    group = layer // 2
    groups = layers // 2
    step = 2 * x - 1
    place = jnp.where(x == 1, group, groups - 1 - group)
    blocks, size, r = chalf.shape
    count = tiles.shape[0]
    mine = pl.multiple_of((1 - x) * r, r)
    other = pl.multiple_of(x * r, r)
    first = place == 0
    last = place == groups - 1
    odd = lax.rem(place, 2) == 1
    middle = jnp.logical_not(odd | first)
    twin = lat + 1 - 2 * lax.rem(lat, 2)
    partner_lat = jnp.where(middle, twin, lat)
    next_lat = jnp.where(place == groups - 2, lat, twin)

    def others(visit, downward):
        def visit_layer(i):
            to = layers - 1 - i if downward else i

            for across in range(1, lateral):
                visit(to, wrap(lat + across, lateral))

            @pl.when(to != layer)
            def _():
                visit(to, lat)

        if devices == GROUP:
            for i in range(layers):
                visit_layer(i)
        else:
            pl.loop(0, layers)(visit_layer)

    def wrap(index, length):
        return jnp.where(index >= length, index - length, index)

    smalls = [
        pltpu.make_async_copy(source, target, small_sem.at[i])
        for i, (source, target) in enumerate(((tiles_in, tiles), (dest_in, dest), (code_in, code)))
    ]
    for load in smalls:
        load.start()
    loads = [
        pltpu.make_async_copy(inv.at[0, :, :, pl.ds(mine, r)], chalf, load_sem.at[0]),
        pltpu.make_async_copy(inv.at[0, :, :, pl.ds(other, r)], ohalf, load_sem.at[1]),
    ]
    for load in loads:
        load.start()

    barrier = pltpu.get_barrier_semaphore()

    def greet(to_layer, to_lat):
        pl.semaphore_signal(
            barrier, inc=1, device_id=(to_layer, to_lat), device_id_type=MESH
        )

    others(greet, False)

    for load in smalls:
        load.wait()

    row_t = lax.broadcasted_iota(jnp.int32, (count, count), 0)
    col_t = lax.broadcasted_iota(jnp.int32, (count, count), 1)
    target = dest[...]
    across = jnp.broadcast_to(target, (count, count))
    named = jnp.sum(jnp.where(row_t == col_t, across, 0), axis=1, keepdims=True)
    order = jnp.sum(
        jnp.where((named == target) & (row_t < col_t), 1, 0), axis=0, keepdims=True
    )
    codes = jnp.broadcast_to(code[...], (count, count)) + 1
    code_col = jnp.sum(jnp.where(row_t == col_t, codes, 0), axis=1, keepdims=True)
    half = r // 2
    parts = [
        tiles[:, :half],
        tiles[:, half:],
        jnp.broadcast_to(code_col, (count, half)).astype(F32).astype(BF16),
    ]
    shape_w = (GROUP * 8, count)
    row_w = lax.broadcasted_iota(jnp.int32, shape_w, 0)
    q_w = row_w % 8
    slot_w = jnp.where(q_w < 4, q_w // 2, q_w - 4)
    kind_w = jnp.where(q_w < 4, q_w % 2, jnp.where(q_w < 6, 2, 3))

    def pack(chunk):
        hit = (target == chunk * GROUP + row_w // 8) & (order == slot_w)
        message = jnp.zeros((GROUP * 8, half), F32)
        for kind, part in enumerate(parts):
            picks = jnp.where(hit & (kind_w == kind), 1.0, 0.0).astype(BF16)
            message = message + jnp.dot(picks, part, preferred_element_type=F32)
        send[pl.ds(chunk * GROUP, GROUP)] = message.reshape(GROUP, 8, half).astype(BF16)

    if devices == GROUP:
        pack(0)
    else:
        pl.loop(0, devices // GROUP)(pack)
    recv[me] = send[me]

    pl.semaphore_wait(barrier, devices - 1)

    def route(to_layer, to_lat):
        pltpu.make_async_remote_copy(
            src_ref=send.at[to_layer * lateral + to_lat],
            dst_ref=recv.at[me],
            send_sem=send_sem,
            recv_sem=recv_sem,
            device_id=(to_layer, to_lat),
            device_id_type=MESH,
        ).start()

    def copy(source, target, send_at, recv_at, to, to_lat):
        return pltpu.make_async_remote_copy(
            src_ref=source, dst_ref=target, send_sem=send_at, recv_sem=recv_at,
            device_id=(to, to_lat), device_id_type=MESH,
        )

    partner = layer - step
    onward = layer + 2 * step
    parts_of = [(b, pl.ds(h, half)) for b in reversed(range(blocks)) for h in range(0, r, half)]
    sent = len(parts_of) - 2
    far_copies = [
        copy(
            inv.at[0, b, pl.ds(mine, r), pl.ds(pl.multiple_of(other + h.start, half), half)],
            far.at[b, :, h], far_send.at[i], far_recv.at[i], partner, partner_lat,
        )
        for i, (b, h) in enumerate(parts_of)
    ]
    raw_copies = [
        copy(
            inv.at[0, b, pl.ds(other, r), pl.ds(pl.multiple_of(mine + h.start, half), half)],
            zfar.at[b, :, h], zfar_send.at[i], zfar_recv.at[i], onward, next_lat,
        )
        for i, (b, h) in enumerate(parts_of)
    ]
    comp_copies = [
        copy(
            comp.at[b, :, h], zfar.at[b, :, h],
            zfar_send.at[i], zfar_recv.at[i], onward, next_lat,
        )
        for i, (b, h) in enumerate(parts_of)
    ]

    head_copy = copy(
        inv.at[0, 0, pl.ds(other, r), pl.ds(mine, r)], head, head_send, head_recv, onward, next_lat
    )
    tail_copy = copy(
        inv.at[0, 0, pl.ds(mine, r), pl.ds(other, r)], tail, tail_send, tail_recv,
        layer - 3 * step, jnp.where(place == 1, lat, twin),
    )

    for across in range(lateral):
        route(partner, wrap(lat + across, lateral))

    @pl.when(jnp.logical_not(first | last))
    def _():
        for far_copy in far_copies:
            far_copy.start()

    def route_far(to_layer, to_lat):
        @pl.when(to_layer != partner)
        def _():
            route(to_layer, to_lat)

    others(route_far, True)

    @pl.when(middle)
    def _():
        head_copy.start()

    @pl.when(odd & jnp.logical_not(last))
    def _():
        tail_copy.start()

    @pl.when(first)
    def _():
        for raw_copy in raw_copies:
            raw_copy.start()

    @pl.when(first)
    def _():
        for far_copy in far_copies:
            far_copy.start()

    for load in loads:
        load.wait()

    u_copy = copy(
        chalf.at[:, pl.ds(other, r), :], usib, u_send, u_recv, layer, twin
    )

    @pl.when(odd & jnp.logical_not(last))
    def _():
        u_copy.start()

    def step_of(b):
        return chalf[b, pl.ds(other, r), :]

    def compose(i):
        b, h = parts_of[i]
        far_copies[i].wait_recv()
        comp[b, :, h] = jnp.dot(
            step_of(b), far[b, :, h], preferred_element_type=F32
        ).astype(BF16)
        if i < sent:
            comp_copies[i].start()

    @pl.when(middle & (x == 0))
    def _():
        for i in range(2):
            compose(i)

    everyone = pl.ds(0, devices - 1)
    pltpu.make_async_copy(recv.at[everyone], recv.at[everyone], recv_sem).wait()

    shape_u = (GROUP, 8, half)
    q_u = lax.broadcasted_iota(jnp.int32, shape_u, 1)
    lane = lax.broadcasted_iota(jnp.int32, shape_u, 2)
    s_of, half_of, plane_of, block_of = lane % 8, (lane // 8) % 2, (lane // 16) % 2, lane // 32
    wanted = (((s_of * 2 + plane_of) * blocks + block_of) + 1).astype(F32)
    usable = (q_u < 4) & (q_u % 2 == half_of) & (lane < 64)

    def unpack(chunk):
        got = recv[pl.ds(chunk * GROUP, GROUP)].astype(F32)
        named_code = jnp.where(q_u < 2, got[:, 4:5, :], got[:, 5:6, :])
        table = jnp.where(usable & (named_code == wanted), 1.0, 0.0)
        return lax.dot_general(
            table.reshape(GROUP * 8, half).astype(BF16),
            got.reshape(GROUP * 8, half).astype(BF16),
            (((0,), (0,)), ((), ())),
            preferred_element_type=F32,
        )

    if devices == GROUP:
        field = unpack(0)
    else:
        field = lax.fori_loop(
            0, devices // GROUP, lambda i, total: total + unpack(i), jnp.zeros((half, half), F32)
        )

    upper = x == 1
    for b in range(blocks):
        rows = [field[32 * b + 8 * k : 32 * b + 8 * k + 8] for k in range(4)]
        top = jnp.concatenate(rows[:2], axis=1)
        bottom = jnp.concatenate(rows[2:], axis=1)
        own = jnp.where(upper, top, bottom).astype(BF16)
        away = jnp.where(upper, bottom, top).astype(BF16)
        local = nt(own, chalf[b]) + nt(away, ohalf[b])
        acc[b] = local
        give[b] = jnp.where(upper, local[:, :r], local[:, r:]).astype(BF16)
        owned = jnp.where(upper, local[:, r:], local[:, :r])
        base[b] = owned
        qout[b] = owned.astype(BF16)

    po_copy = copy(give, po, po_send, po_recv, partner, partner_lat)
    start_copy = copy(
        give, cin, t_send, c_recv, layer - 3 * step, lat if groups == 2 else twin
    )
    q_copy = copy(qout, qin, q_send, q_recv, onward, next_lat)
    far_lat = jnp.where(place == groups - 3, twin, lat)
    c_copies = [
        copy(fout, cin, c_send.at[0], c_recv, onward, twin),
        copy(fout, cin, c_send.at[1], c_recv, layer + 4 * step, far_lat),
    ]
    o_copy = copy(fout, oin, o_send, o_recv, layer + step, jnp.where(odd, twin, lat))
    own_copy = copy(qout, osib, own_send, own_recv, layer, twin)
    trace_copy = copy(tout, tin, trace_send, trace_recv, layer, twin)

    @pl.when(odd & jnp.logical_not(last))
    def _():
        own_copy.start()

    @pl.when(last)
    def _():
        start_copy.start()

    po_copy.start()

    @pl.when(first)
    def _():
        q_copy.start()

    def opposite():
        o_copy.wait_recv()
        for b in range(blocks):
            acc[b] = acc[b] + nt(oin[b], ohalf[b])

    @pl.when(first)
    def _():
        po_copy.wait_recv()
        for b in range(blocks):
            fout[b] = (nt(po[b], step_of(b)) + base[b]).astype(BF16)
        o_copy.start()
        for b in range(blocks):
            acc[b] = acc[b] + nt(po[b], chalf[b])
        opposite()

    @pl.when(middle)
    def _():
        @pl.when(x == 1)
        def _():
            for i in range(2):
                compose(i)

        for i in range(2, len(parts_of)):
            compose(i)
        po_copy.wait_recv()
        for b in range(blocks):
            total = nt(po[b], step_of(b)) + base[b]
            base[b] = total
            qout[b] = total.astype(BF16)
        q_copy.start()

        def chain():
            c_copies[0].wait_recv()
            for b in range(blocks):
                fout[b] = (nt(cin[b], comp[b]) + base[b]).astype(BF16)
            o_copy.start()
            for b in range(blocks):
                trace = nt(cin[b], far[b]) + po[b].astype(F32)
                acc[b] = acc[b] + nt(trace.astype(BF16), chalf[b])

        early = 2 * place < groups

        @pl.when(early)
        def _():
            chain()
            opposite()

        @pl.when(jnp.logical_not(early))
        def _():
            opposite()
            chain()

    @pl.when(odd)
    def _():
        for i in range(len(parts_of)):
            far_copies[i].wait_recv()
        for i in range(sent):
            comp_copies[i].wait_recv()

        @pl.when(place == 1)
        def _():
            for i in range(sent, len(parts_of)):
                comp_copies[i].wait_recv()

        @pl.when(place > 1)
        def _():
            head_copy.wait_recv()
            tail_copy.wait_recv()
            zfar[0] = jnp.dot(head[...], tail[...], preferred_element_type=F32).astype(BF16)

        po_copy.wait_recv()
        q_copy.wait_recv()
        c_copies[0].wait_recv()
        traces = []
        for b in range(blocks):
            between = nt(cin[b], zfar[b]) + qin[b].astype(F32)
            traces.append((nt(between.astype(BF16), far[b]) + po[b].astype(F32)).astype(BF16))

        @pl.when(last)
        def _():
            for b in range(blocks):
                acc[b] = acc[b] + nt(traces[b], chalf[b])

        @pl.when(jnp.logical_not(last))
        def _():
            u_copy.wait_recv()
            own_copy.wait_recv()
            for b in range(blocks):
                fout[b] = (nt(traces[b], usib[b]) + osib[b].astype(F32)).astype(BF16)
                tout[b] = traces[b]
            c_copies[1].start()
            c_copies[0].start()
            o_copy.start()
            trace_copy.start()
            trace_copy.wait_recv()
            for b in range(blocks):
                acc[b] = acc[b] + nt(tin[b], chalf[b])
            opposite()

    for b in range(blocks):
        out[0, b] = acc[b]

    @pl.when(jnp.logical_not(last))
    def _():
        for far_copy in far_copies:
            far_copy.wait_send()
        o_copy.wait_send()

    @pl.when(last)
    def _():
        start_copy.wait_send()

    @pl.when(first)
    def _():
        for comp_copy in comp_copies[sent:]:
            comp_copy.wait_send()

    @pl.when(middle)
    def _():
        head_copy.wait_send()

    @pl.when(jnp.logical_not(odd))
    def _():
        for comp_copy in comp_copies[:sent]:
            comp_copy.wait_send()
        q_copy.wait_send()

    @pl.when(odd & jnp.logical_not(last))
    def _():
        for c_copy in [*c_copies, u_copy, own_copy, trace_copy, tail_copy]:
            c_copy.wait_send()

    po_copy.wait_send()
    pltpu.make_async_copy(send.at[everyone], send.at[everyone], send_sem).wait()


def body(layers, lateral, inverse, tiles, tile_dest, tile_code):
    devices = layers * lateral
    _, blocks, size, _ = inverse.shape
    r = tiles.shape[1]
    src = 8
    dma = pltpu.SemaphoreType.DMA
    small = (blocks, src, r)
    matrix = pltpu.VMEM((blocks, r, r), BF16)
    vmem = pl.BlockSpec(memory_space=pltpu.VMEM)
    return pl.pallas_call(
        functools.partial(kernel, layers, lateral),
        out_shape=jax.ShapeDtypeStruct((1, blocks, src, size), F32),
        in_specs=[pl.BlockSpec(memory_space=pltpu.HBM)] * 4,
        out_specs=vmem,
        scratch_shapes=[
            pltpu.VMEM(tiles.shape, BF16),
            pltpu.VMEM((1, tiles.shape[0]), jnp.int32),
            pltpu.VMEM((1, tiles.shape[0]), jnp.int32),
            pltpu.VMEM((devices, 8, r // 2), BF16),
            pltpu.VMEM((devices, 8, r // 2), BF16),
            pltpu.VMEM((blocks, size, r), BF16),
            pltpu.VMEM((blocks, size, r), BF16),
            matrix, matrix, matrix,
            pltpu.VMEM((blocks, src, size), F32),
            pltpu.VMEM(small, F32),
        ]
        + [pltpu.VMEM(small, BF16)] * 7
        + [matrix]
        + [pltpu.VMEM(small, BF16)] * 3
        + [pltpu.VMEM((r, r), BF16)] * 2
        + [dma((3,)), dma((2,)), dma, dma]
        + [dma((2 * blocks,))] * 4
        + [dma] * 3
        + [dma((2,))]
        + [dma] * 15,
        compiler_params=pltpu.CompilerParams(
            collective_id=0, has_side_effects=True, vmem_limit_bytes=48 * 1024 * 1024
        ),
        name="sweep",
    )(
        *(
            pltpu.with_memory_space_constraint(array, pltpu.HBM)
            for array in (inverse, tiles, tile_dest.reshape(1, -1), tile_code.reshape(1, -1))
        )
    )


def solution(mesh):
    in_specs = (
        P("layer", "lat", None, None),
        P(("layer", "lat"), None),
        P(("layer", "lat"), None),
        P(("layer", "lat")),
    )
    out_specs = P("layer", "lat", None, None)
    return jax.shard_map(
        functools.partial(body, mesh.shape["layer"], mesh.shape["lat"]),
        mesh=mesh, in_specs=in_specs, out_specs=out_specs, check_vma=False,
    )
```

```python
import functools

import jax
import jax.numpy as jnp
from jax import lax
from jax.experimental import pallas as pl
from jax.experimental.pallas import tpu as pltpu
from jax.sharding import PartitionSpec as P

MESH = pl.DeviceIdType.MESH
F32 = jnp.float32
BF16 = jnp.bfloat16
GROUP = 32


def nt(vectors, matrix):
    return lax.dot_general(vectors, matrix, (((1,), (1,)), ((), ())), preferred_element_type=F32)


def kernel(
    layers, lateral,
    inv, tiles_in, dest_in, code_in, out,
    tiles, dest, code, send, recv, chalf, ohalf, far, zfar, comp, acc, base, give, po, cin, oin, qin, qout, fout, usib, osib, tout, tin, head, tail,
    small_sem, load_sem, send_sem, recv_sem, far_send, far_recv, zfar_send, zfar_recv,
    po_send, po_recv, t_send, c_send, c_recv, o_send, o_recv, q_send, q_recv,
    head_send, head_recv, tail_send, tail_recv, u_send, u_recv, own_send, own_recv, trace_send, trace_recv,
):
    layer = lax.axis_index("layer")
    lat = lax.axis_index("lat")
    devices = layers * lateral
    me = layer * lateral + lat
    x = lax.rem(layer, 2)
    group = layer // 2
    groups = layers // 2
    step = 2 * x - 1
    place = jnp.where(x == 1, group, groups - 1 - group)
    blocks, size, r = chalf.shape
    count = tiles.shape[0]
    mine = pl.multiple_of((1 - x) * r, r)
    other = pl.multiple_of(x * r, r)
    first = place == 0
    last = place == groups - 1
    odd = lax.rem(place, 2) == 1
    middle = jnp.logical_not(odd | first)
    twin = lat + 1 - 2 * lax.rem(lat, 2)
    partner_lat = jnp.where(middle, twin, lat)
    upper_core = lax.rem(lat, 2) == 1
    next_lat = jnp.where(place == groups - 2, lat, twin)

    def others(visit, pick, begin, end):
        def visit_layer(i):
            to = pick(i)

            for across in range(1, lateral):
                visit(to, wrap(lat + across, lateral))

            @pl.when(to != layer)
            def _():
                visit(to, lat)

        if devices == GROUP:
            for i in range(begin, end):
                visit_layer(i)
        else:
            pl.loop(begin, end)(visit_layer)

    def wrap(index, length):
        return jnp.where(index >= length, index - length, index)

    smalls = [
        pltpu.make_async_copy(source, target, small_sem.at[i])
        for i, (source, target) in enumerate(((tiles_in, tiles), (dest_in, dest), (code_in, code)))
    ]
    for load in smalls:
        load.start()
    loads = [
        pltpu.make_async_copy(inv.at[0, :, :, pl.ds(mine, r)], chalf, load_sem.at[0]),
        pltpu.make_async_copy(inv.at[0, :, :, pl.ds(other, r)], ohalf, load_sem.at[1]),
    ]
    for load in loads:
        load.start()

    barrier = pltpu.get_barrier_semaphore()

    def greet(to_layer, to_lat):
        pl.semaphore_signal(
            barrier, inc=1, device_id=(to_layer, to_lat), device_id_type=MESH
        )

    others(greet, lambda i: i, 0, layers)

    for load in smalls:
        load.wait()

    row_t = lax.broadcasted_iota(jnp.int32, (count, count), 0)
    col_t = lax.broadcasted_iota(jnp.int32, (count, count), 1)
    target = dest[...]
    across = jnp.broadcast_to(target, (count, count))
    named = jnp.sum(jnp.where(row_t == col_t, across, 0), axis=1, keepdims=True)
    order = jnp.sum(
        jnp.where((named == target) & (row_t < col_t), 1, 0), axis=0, keepdims=True
    )
    codes = jnp.broadcast_to(code[...], (count, count)) + 1
    code_col = jnp.sum(jnp.where(row_t == col_t, codes, 0), axis=1, keepdims=True)
    half = r // 2
    parts = [
        tiles[:, :half],
        tiles[:, half:],
        jnp.broadcast_to(code_col, (count, half)).astype(F32).astype(BF16),
    ]
    shape_w = (GROUP * 8, count)
    row_w = lax.broadcasted_iota(jnp.int32, shape_w, 0)
    q_w = row_w % 8
    slot_w = jnp.where(q_w < 4, q_w // 2, q_w - 4)
    kind_w = jnp.where(q_w < 4, q_w % 2, jnp.where(q_w < 6, 2, 3))

    def pack(chunk):
        hit = (target == chunk * GROUP + row_w // 8) & (order == slot_w)
        message = jnp.zeros((GROUP * 8, half), F32)
        for kind, part in enumerate(parts):
            picks = jnp.where(hit & (kind_w == kind), 1.0, 0.0).astype(BF16)
            message = message + jnp.dot(picks, part, preferred_element_type=F32)
        send[pl.ds(chunk * GROUP, GROUP)] = message.reshape(GROUP, 8, half).astype(BF16)

    if devices == GROUP:
        pack(0)
    else:
        pl.loop(0, devices // GROUP)(pack)
    recv[me] = send[me]

    pl.semaphore_wait(barrier, devices - 1)

    def route(to_layer, to_lat):
        pltpu.make_async_remote_copy(
            src_ref=send.at[to_layer * lateral + to_lat],
            dst_ref=recv.at[me],
            send_sem=send_sem,
            recv_sem=recv_sem,
            device_id=(to_layer, to_lat),
            device_id_type=MESH,
        ).start()

    def copy(source, target, send_at, recv_at, to, to_lat):
        return pltpu.make_async_remote_copy(
            src_ref=source, dst_ref=target, send_sem=send_at, recv_sem=recv_at,
            device_id=(to, to_lat), device_id_type=MESH,
        )

    partner = layer - step
    onward = layer + 2 * step
    parts_of = [(b, pl.ds(h, half)) for b in reversed(range(blocks)) for h in range(0, r, half)]
    sent = len(parts_of) - 1
    far_copies = [
        copy(
            inv.at[0, b, pl.ds(mine, r), pl.ds(pl.multiple_of(other + h.start, half), half)],
            far.at[b, :, h], far_send.at[i], far_recv.at[i], partner, partner_lat,
        )
        for i, (b, h) in enumerate(parts_of)
    ]
    raw_copies = [
        copy(
            inv.at[0, b, pl.ds(other, r), pl.ds(pl.multiple_of(mine + h.start, half), half)],
            zfar.at[b, :, h], zfar_send.at[i], zfar_recv.at[i], onward, next_lat,
        )
        for i, (b, h) in enumerate(parts_of)
    ]
    comp_copies = [
        copy(
            comp.at[b, :, h], zfar.at[b, :, h],
            zfar_send.at[i], zfar_recv.at[i], onward, next_lat,
        )
        for i, (b, h) in enumerate(parts_of)
    ]

    end = parts_of[-1][1]
    head_copy = copy(
        inv.at[0, 0, pl.ds(other, r), pl.ds(mine, r)], head, head_send, head_recv, onward, next_lat
    )
    tail_copy = copy(
        inv.at[0, 0, pl.ds(mine, r), pl.ds(pl.multiple_of(other + end.start, half), half)],
        tail, tail_send, tail_recv,
        layer - 3 * step, jnp.where(place == 1, lat, twin),
    )

    turned = first & (x == 0)

    @pl.when(jnp.logical_not(turned))
    def _():
        for across in range(lateral):
            route(partner, wrap(lat + across, lateral))

    @pl.when(jnp.where(first, x == 1, jnp.logical_not(last)))
    def _():
        for far_copy in far_copies:
            far_copy.start()

    def route_far(to_layer, to_lat):
        @pl.when(turned | (to_layer != partner))
        def _():
            route(to_layer, to_lat)

    def downward(i):
        at = jnp.where(turned, layers - 3, layers - 1) - i
        return jnp.where(at < 0, at + layers, at)

    others(route_far, downward, 0, layers - 2)

    @pl.when(first)
    def _():
        for raw_copy in raw_copies:
            raw_copy.start()

    others(route_far, downward, layers - 2, layers)

    @pl.when(middle)
    def _():
        head_copy.start()

    @pl.when(odd & jnp.logical_not(last))
    def _():
        tail_copy.start()

    @pl.when(turned)
    def _():
        for far_copy in far_copies:
            far_copy.start()

    for load in loads:
        load.wait()

    u_copy = copy(
        chalf.at[:, pl.ds(other, r), :], usib, u_send, u_recv, layer, twin
    )

    @pl.when(odd & jnp.logical_not(last))
    def _():
        u_copy.start()

    def step_of(b):
        return chalf[b, pl.ds(other, r), :]

    def compose(i):
        b, h = parts_of[i]
        far_copies[i].wait_recv()
        comp[b, :, h] = jnp.dot(
            step_of(b), far[b, :, h], preferred_element_type=F32
        ).astype(BF16)
        if i < sent:
            comp_copies[i].start()

    @pl.when(middle & (x == 0))
    def _():
        for i in range(2):
            compose(i)

    everyone = pl.ds(0, devices - 1)
    pltpu.make_async_copy(recv.at[everyone], recv.at[everyone], recv_sem).wait()

    shape_u = (GROUP, 8, half)
    q_u = lax.broadcasted_iota(jnp.int32, shape_u, 1)
    lane = lax.broadcasted_iota(jnp.int32, shape_u, 2)
    s_of, half_of, plane_of, block_of = lane % 8, (lane // 8) % 2, (lane // 16) % 2, lane // 32
    wanted = (((s_of * 2 + plane_of) * blocks + block_of) + 1).astype(F32)
    usable = (q_u < 4) & (q_u % 2 == half_of) & (lane < 64)

    def unpack(chunk):
        got = recv[pl.ds(chunk * GROUP, GROUP)].astype(F32)
        named_code = jnp.where(q_u < 2, got[:, 4:5, :], got[:, 5:6, :])
        table = jnp.where(usable & (named_code == wanted), 1.0, 0.0)
        return lax.dot_general(
            table.reshape(GROUP * 8, half).astype(BF16),
            got.reshape(GROUP * 8, half).astype(BF16),
            (((0,), (0,)), ((), ())),
            preferred_element_type=F32,
        )

    if devices == GROUP:
        field = unpack(0)
    else:
        field = lax.fori_loop(
            0, devices // GROUP, lambda i, total: total + unpack(i), jnp.zeros((half, half), F32)
        )

    upper = x == 1
    for b in range(blocks):
        rows = [field[32 * b + 8 * k : 32 * b + 8 * k + 8] for k in range(4)]
        top = jnp.concatenate(rows[:2], axis=1)
        bottom = jnp.concatenate(rows[2:], axis=1)
        own = jnp.where(upper, top, bottom).astype(BF16)
        away = jnp.where(upper, bottom, top).astype(BF16)
        local = nt(own, chalf[b]) + nt(away, ohalf[b])
        acc[b] = local
        give[b] = jnp.where(upper, local[:, :r], local[:, r:]).astype(BF16)
        owned = jnp.where(upper, local[:, r:], local[:, :r])
        base[b] = owned
        qout[b] = owned.astype(BF16)

    po_copy = copy(give, po, po_send, po_recv, partner, partner_lat)
    start_copy = copy(
        give, cin, t_send, c_recv, layer - 3 * step, lat if groups == 2 else twin
    )
    q_copy = copy(qout, qin, q_send, q_recv, onward, next_lat)
    far_lat = jnp.where(place == groups - 3, twin, lat)
    c_copies = [
        copy(fout, cin, c_send.at[0], c_recv, onward, twin),
        copy(fout, cin, c_send.at[1], c_recv, layer + 4 * step, far_lat),
    ]
    o_copy = copy(fout, oin, o_send, o_recv, layer + step, jnp.where(odd, twin, lat))
    own_copy = copy(qout, osib, own_send, own_recv, layer, twin)
    both_copy = copy(fout, tin, c_send.at[2], trace_recv, onward, lat)
    hand_copy = copy(comp, usib, u_send, u_recv, layer, twin)
    twin_copy = copy(tout, oin, trace_send, o_recv, layer + step, twin)
    trace_copy = copy(tout, tin, trace_send, trace_recv, layer, twin)

    @pl.when(odd & jnp.logical_not(last))
    def _():
        own_copy.start()

    @pl.when(last)
    def _():
        start_copy.start()

    po_copy.start()

    @pl.when(first)
    def _():
        q_copy.start()

    def opposite():
        o_copy.wait_recv()
        for b in range(blocks):
            acc[b] = acc[b] + nt(oin[b], ohalf[b])

    @pl.when(first)
    def _():
        po_copy.wait_recv()
        for b in range(blocks):
            fout[b] = (nt(po[b], step_of(b)) + base[b]).astype(BF16)
        o_copy.start()
        for b in range(blocks):
            acc[b] = acc[b] + nt(po[b], chalf[b])
        opposite()

    @pl.when(middle)
    def _():
        @pl.when(x == 1)
        def _():
            for i in range(2):
                compose(i)

        for i in range(2, len(parts_of)):
            compose(i)

        @pl.when(jnp.logical_not(upper_core))
        def _():
            hand_copy.start()

        po_copy.wait_recv()
        for b in range(blocks):
            total = nt(po[b], step_of(b)) + base[b]
            base[b] = total
            qout[b] = total.astype(BF16)
        q_copy.start()

        @pl.when(jnp.logical_not(upper_core))
        def _():
            own_copy.start()
            c_copies[0].wait_recv()

        @pl.when(upper_core)
        def _():
            hand_copy.wait_recv()
            own_copy.wait_recv()
            both_copy.wait_recv()
            for b in range(blocks):
                tout[b] = (nt(tin[b], usib[b]) + osib[b].astype(F32)).astype(BF16)
            twin_copy.start()
            c_copies[0].wait_recv()
            for b in range(blocks):
                fout[b] = (nt(cin[b], comp[b]) + base[b]).astype(BF16)
            o_copy.start()

        for b in range(blocks):
            trace = nt(cin[b], far[b]) + po[b].astype(F32)
            acc[b] = acc[b] + nt(trace.astype(BF16), chalf[b])
        opposite()

    def steps():
        for i in range(sent):
            comp_copies[i].wait_recv()

        @pl.when(place == 1)
        def _():
            for i in range(sent, len(parts_of)):
                comp_copies[i].wait_recv()

        @pl.when(place > 1)
        def _():
            head_copy.wait_recv()
            tail_copy.wait_recv()
            zfar[0, :, end] = jnp.dot(
                head[...], tail[...], preferred_element_type=F32
            ).astype(BF16)

    @pl.when(last)
    def _():
        for far_copy in far_copies:
            far_copy.wait_recv()
        steps()
        po_copy.wait_recv()
        q_copy.wait_recv()
        c_copies[0].wait_recv()
        for b in range(blocks):
            between = nt(cin[b], zfar[b]) + qin[b].astype(F32)
            trace = nt(between.astype(BF16), far[b]) + po[b].astype(F32)
            acc[b] = acc[b] + nt(trace.astype(BF16), chalf[b])

    @pl.when(odd & jnp.logical_not(last))
    def _():
        u_copy.wait_recv()
        for i, (b, h) in enumerate(parts_of):
            far_copies[i].wait_recv()
            comp[b, :, h] = jnp.dot(
                usib[b], far[b, :, h], preferred_element_type=F32
            ).astype(BF16)
        po_copy.wait_recv()
        own_copy.wait_recv()
        rest = [nt(po[b], usib[b]) + osib[b].astype(F32) for b in range(blocks)]
        steps()
        q_copy.wait_recv()
        c_copies[0].wait_recv()
        middles = []
        for b in range(blocks):
            between = (nt(cin[b], zfar[b]) + qin[b].astype(F32)).astype(BF16)
            fout[b] = (nt(between, comp[b]) + rest[b]).astype(BF16)
            middles.append(between)
        @pl.when(upper_core)
        def _():
            both_copy.start()

        c_copies[0].start()
        c_copies[1].start()
        o_copy.start()
        for b in range(blocks):
            tout[b] = (nt(middles[b], far[b]) + po[b].astype(F32)).astype(BF16)
        trace_copy.start()
        trace_copy.wait_recv()
        for b in range(blocks):
            acc[b] = acc[b] + nt(tin[b], chalf[b])
        opposite()

    for b in range(blocks):
        out[0, b] = acc[b]

    @pl.when(jnp.logical_not(last))
    def _():
        for far_copy in far_copies:
            far_copy.wait_send()

    @pl.when(last)
    def _():
        start_copy.wait_send()

    @pl.when(first)
    def _():
        for comp_copy in comp_copies[sent:]:
            comp_copy.wait_send()

    @pl.when(middle)
    def _():
        head_copy.wait_send()

        @pl.when(upper_core)
        def _():
            twin_copy.wait_send()

        @pl.when(jnp.logical_not(upper_core))
        def _():
            hand_copy.wait_send()
            own_copy.wait_send()

    @pl.when(odd & jnp.logical_not(last) & upper_core)
    def _():
        both_copy.wait_send()

    @pl.when(jnp.logical_not(last | (middle & jnp.logical_not(upper_core))))
    def _():
        o_copy.wait_send()

    @pl.when(jnp.logical_not(odd))
    def _():
        for comp_copy in comp_copies[:sent]:
            comp_copy.wait_send()
        q_copy.wait_send()

    @pl.when(odd & jnp.logical_not(last))
    def _():
        for c_copy in [*c_copies, u_copy, own_copy, trace_copy, tail_copy]:
            c_copy.wait_send()

    po_copy.wait_send()
    pltpu.make_async_copy(send.at[everyone], send.at[everyone], send_sem).wait()


def body(layers, lateral, inverse, tiles, tile_dest, tile_code):
    devices = layers * lateral
    _, blocks, size, _ = inverse.shape
    r = tiles.shape[1]
    src = 8
    dma = pltpu.SemaphoreType.DMA
    small = (blocks, src, r)
    matrix = pltpu.VMEM((blocks, r, r), BF16)
    vmem = pl.BlockSpec(memory_space=pltpu.VMEM)
    return pl.pallas_call(
        functools.partial(kernel, layers, lateral),
        out_shape=jax.ShapeDtypeStruct((1, blocks, src, size), F32),
        in_specs=[pl.BlockSpec(memory_space=pltpu.HBM)] * 4,
        out_specs=vmem,
        scratch_shapes=[
            pltpu.VMEM(tiles.shape, BF16),
            pltpu.VMEM((1, tiles.shape[0]), jnp.int32),
            pltpu.VMEM((1, tiles.shape[0]), jnp.int32),
            pltpu.VMEM((devices, 8, r // 2), BF16),
            pltpu.VMEM((devices, 8, r // 2), BF16),
            pltpu.VMEM((blocks, size, r), BF16),
            pltpu.VMEM((blocks, size, r), BF16),
            matrix, matrix, matrix,
            pltpu.VMEM((blocks, src, size), F32),
            pltpu.VMEM(small, F32),
        ]
        + [pltpu.VMEM(small, BF16)] * 7
        + [matrix]
        + [pltpu.VMEM(small, BF16)] * 3
        + [pltpu.VMEM((r, r), BF16), pltpu.VMEM((r, r // 2), BF16)]
        + [dma((3,)), dma((2,)), dma, dma]
        + [dma((2 * blocks,))] * 4
        + [dma] * 3
        + [dma((3,))]
        + [dma] * 15,
        compiler_params=pltpu.CompilerParams(
            collective_id=0, has_side_effects=True, vmem_limit_bytes=48 * 1024 * 1024
        ),
        name="sweep",
    )(
        *(
            pltpu.with_memory_space_constraint(array, pltpu.HBM)
            for array in (inverse, tiles, tile_dest.reshape(1, -1), tile_code.reshape(1, -1))
        )
    )


def solution(mesh):
    in_specs = (
        P("layer", "lat", None, None),
        P(("layer", "lat"), None),
        P(("layer", "lat"), None),
        P(("layer", "lat")),
    )
    out_specs = P("layer", "lat", None, None)
    return jax.shard_map(
        functools.partial(body, mesh.shape["layer"], mesh.shape["lat"]),
        mesh=mesh, in_specs=in_specs, out_specs=out_specs, check_vma=False,
    )
```

```python
import functools

import jax
import jax.numpy as jnp
from jax import lax
from jax.experimental import pallas as pl
from jax.experimental.pallas import tpu as pltpu
from jax.sharding import PartitionSpec as P

MESH = pl.DeviceIdType.MESH
F32 = jnp.float32
BF16 = jnp.bfloat16
GROUP = 32
BATCH = 16


def nt(vectors, matrix):
    return lax.dot_general(vectors, matrix, (((1,), (1,)), ((), ())), preferred_element_type=F32)


def kernel(
    layers, lateral,
    inv, tiles_in, dest_in, code_in, out,
    tiles, dest, code, send, recv, chalf, ohalf, far, zfar, comp, acc, base, give, po, cin, oin, qin, qout, fout, usib, osib, tout, tin, head, tail,
    small_sem, load_sem, send_sem, recv_sem, far_send, far_recv, zfar_send, zfar_recv,
    po_send, po_recv, t_send, c_send, c_recv, o_send, o_recv, q_send, q_recv,
    head_send, head_recv, tail_send, tail_recv, u_send, u_recv, own_send, own_recv, trace_send, trace_recv,
):
    layer = lax.axis_index("layer")
    lat = lax.axis_index("lat")
    devices = layers * lateral
    me = layer * lateral + lat
    x = lax.rem(layer, 2)
    group = layer // 2
    groups = layers // 2
    step = 2 * x - 1
    place = jnp.where(x == 1, group, groups - 1 - group)
    blocks, size, r = chalf.shape
    count = tiles.shape[0]
    mine = pl.multiple_of((1 - x) * r, r)
    other = pl.multiple_of(x * r, r)
    first = place == 0
    last = place == groups - 1
    odd = lax.rem(place, 2) == 1
    middle = jnp.logical_not(odd | first)
    twin = lat + 1 - 2 * lax.rem(lat, 2)
    partner_lat = jnp.where(middle, twin, lat)
    upper_core = lax.rem(lat, 2) == 1
    next_lat = jnp.where(place == groups - 2, lat, twin)

    def others(visit, pick, begin, end):
        def visit_layer(i):
            to = pick(i)

            for across in range(1, lateral):
                visit(to, wrap(lat + across, lateral))

            @pl.when(to != layer)
            def _():
                visit(to, lat)

        if devices == GROUP:
            for i in range(begin, end):
                visit_layer(i)
        else:
            pl.loop(begin, end)(visit_layer)

    def wrap(index, length):
        return jnp.where(index >= length, index - length, index)

    smalls = [
        pltpu.make_async_copy(source, target, small_sem.at[i])
        for i, (source, target) in enumerate(((tiles_in, tiles), (dest_in, dest), (code_in, code)))
    ]
    for load in smalls:
        load.start()
    loads = [
        pltpu.make_async_copy(inv.at[0, :, :, pl.ds(mine, r)], chalf, load_sem.at[0]),
        pltpu.make_async_copy(inv.at[0, :, :, pl.ds(other, r)], ohalf, load_sem.at[1]),
    ]
    for load in loads:
        load.start()

    barrier = pltpu.get_barrier_semaphore()

    def greet(to_layer, to_lat):
        pl.semaphore_signal(
            barrier, inc=1, device_id=(to_layer, to_lat), device_id_type=MESH
        )

    others(greet, lambda i: i, 0, layers)

    for load in smalls:
        load.wait()

    row_t = lax.broadcasted_iota(jnp.int32, (count, count), 0)
    col_t = lax.broadcasted_iota(jnp.int32, (count, count), 1)
    target = dest[...]
    across = jnp.broadcast_to(target, (count, count))
    named = jnp.sum(jnp.where(row_t == col_t, across, 0), axis=1, keepdims=True)
    order = jnp.sum(
        jnp.where((named == target) & (row_t < col_t), 1, 0), axis=0, keepdims=True
    )
    codes = jnp.broadcast_to(code[...], (count, count)) + 1
    code_col = jnp.sum(jnp.where(row_t == col_t, codes, 0), axis=1, keepdims=True)
    half = r // 2
    parts = [
        tiles[:, :half],
        tiles[:, half:],
        jnp.broadcast_to(code_col, (count, half)).astype(F32).astype(BF16),
    ]
    shape_w = (GROUP * 8, count)
    row_w = lax.broadcasted_iota(jnp.int32, shape_w, 0)
    q_w = row_w % 8
    slot_w = jnp.where(q_w < 4, q_w // 2, q_w - 4)
    kind_w = jnp.where(q_w < 4, q_w % 2, jnp.where(q_w < 6, 2, 3))

    def pack(chunk):
        hit = (target == chunk * GROUP + row_w // 8) & (order == slot_w)
        message = jnp.zeros((GROUP * 8, half), F32)
        for kind, part in enumerate(parts):
            picks = jnp.where(hit & (kind_w == kind), 1.0, 0.0).astype(BF16)
            message = message + jnp.dot(picks, part, preferred_element_type=F32)
        send[pl.ds(chunk * GROUP, GROUP)] = message.reshape(GROUP, 8, half).astype(BF16)

    if devices == GROUP:
        pack(0)
    else:
        pl.loop(0, devices // GROUP)(pack)
    recv[me] = send[me]

    pl.semaphore_wait(barrier, devices - 1)

    side = layer // groups
    side_size = devices // 2

    def route(to_layer, to_lat):
        pltpu.make_async_remote_copy(
            src_ref=send.at[to_layer * lateral + to_lat],
            dst_ref=recv.at[me],
            send_sem=send_sem,
            recv_sem=recv_sem.at[side],
            device_id=(to_layer, to_lat),
            device_id_type=MESH,
        ).start()

    def copy(source, target, send_at, recv_at, to, to_lat):
        return pltpu.make_async_remote_copy(
            src_ref=source, dst_ref=target, send_sem=send_at, recv_sem=recv_at,
            device_id=(to, to_lat), device_id_type=MESH,
        )

    partner = layer - step
    onward = layer + 2 * step
    parts_of = [(b, pl.ds(h, half)) for b in reversed(range(blocks)) for h in range(0, r, half)]
    sent = len(parts_of) - 1
    far_copies = [
        copy(
            inv.at[0, b, pl.ds(mine, r), pl.ds(pl.multiple_of(other + h.start, half), half)],
            far.at[b, :, h], far_send.at[i], far_recv.at[i], partner, partner_lat,
        )
        for i, (b, h) in enumerate(parts_of)
    ]
    raw_copies = [
        copy(
            inv.at[0, b, pl.ds(other, r), pl.ds(pl.multiple_of(mine + h.start, half), half)],
            zfar.at[b, :, h], zfar_send.at[i], zfar_recv.at[i], onward, next_lat,
        )
        for i, (b, h) in enumerate(parts_of)
    ]
    comp_copies = [
        copy(
            comp.at[b, :, h], zfar.at[b, :, h],
            zfar_send.at[i], zfar_recv.at[i], onward, next_lat,
        )
        for i, (b, h) in enumerate(parts_of)
    ]

    end = parts_of[-1][1]
    head_copy = copy(
        inv.at[0, 0, pl.ds(other, r), pl.ds(mine, r)], head, head_send, head_recv, onward, next_lat
    )
    tail_copy = copy(
        inv.at[0, 0, pl.ds(mine, r), pl.ds(pl.multiple_of(other + end.start, half), half)],
        tail, tail_send, tail_recv,
        layer - 3 * step, jnp.where(place == 1, lat, twin),
    )

    turned = first & (x == 0)

    @pl.when(jnp.logical_not(turned))
    def _():
        for across in range(lateral):
            route(partner, wrap(lat + across, lateral))

    @pl.when(jnp.where(first, x == 1, jnp.logical_not(last)))
    def _():
        for far_copy in far_copies:
            far_copy.start()

    def route_far(to_layer, to_lat):
        @pl.when(turned | (to_layer != partner))
        def _():
            route(to_layer, to_lat)

    def downward(i):
        at = jnp.where(turned, layers - 3, layers - 1) - i
        return jnp.where(at < 0, at + layers, at)

    others(route_far, downward, 0, layers - 2)

    @pl.when(first)
    def _():
        for raw_copy in raw_copies:
            raw_copy.start()

    others(route_far, downward, layers - 2, layers)

    @pl.when(middle)
    def _():
        head_copy.start()

    @pl.when(odd & jnp.logical_not(last))
    def _():
        tail_copy.start()

    @pl.when(turned)
    def _():
        for far_copy in far_copies:
            far_copy.start()

    for load in loads:
        load.wait()

    u_copy = copy(
        chalf.at[:, pl.ds(other, r), :], usib, u_send, u_recv, layer, twin
    )

    @pl.when(odd & jnp.logical_not(last))
    def _():
        u_copy.start()

    def step_of(b):
        return chalf[b, pl.ds(other, r), :]

    def compose(i):
        b, h = parts_of[i]
        far_copies[i].wait_recv()
        comp[b, :, h] = jnp.dot(
            step_of(b), far[b, :, h], preferred_element_type=F32
        ).astype(BF16)
        if i < sent:
            comp_copies[i].start()

    @pl.when(middle & (x == 0))
    def _():
        for i in range(2):
            compose(i)

    everyone = pl.ds(0, devices - 1)

    shape_u = (BATCH, 8, half)
    q_u = lax.broadcasted_iota(jnp.int32, shape_u, 1)
    lane = lax.broadcasted_iota(jnp.int32, shape_u, 2)
    s_of, half_of, plane_of, block_of = lane % 8, (lane // 8) % 2, (lane // 16) % 2, lane // 32
    wanted = (((s_of * 2 + plane_of) * blocks + block_of) + 1).astype(F32)
    usable = (q_u < 4) & (q_u % 2 == half_of) & (lane < 64)

    def unpack(begin):
        got = recv[pl.ds(begin, BATCH)].astype(F32)
        named_code = jnp.where(q_u < 2, got[:, 4:5, :], got[:, 5:6, :])
        table = jnp.where(usable & (named_code == wanted), 1.0, 0.0)
        return lax.dot_general(
            table.reshape(BATCH * 8, half).astype(BF16),
            got.reshape(BATCH * 8, half).astype(BF16),
            (((0,), (0,)), ((), ())),
            preferred_element_type=F32,
        )

    def unpack_side(at):
        begin = at * side_size
        if side_size == BATCH:
            return unpack(begin)
        return lax.fori_loop(
            0, side_size // BATCH, lambda i, total: total + unpack(begin + i * BATCH),
            jnp.zeros((half, half), F32),
        )

    near = recv.at[pl.ds(0, side_size - 1)]
    distant = recv.at[pl.ds(0, side_size)]
    pltpu.make_async_copy(near, near, recv_sem.at[side]).wait()
    field = unpack_side(side)
    pltpu.make_async_copy(distant, distant, recv_sem.at[1 - side]).wait()
    field = field + unpack_side(1 - side)

    upper = x == 1
    fields, given = [], []
    for b in range(blocks):
        rows = [field[32 * b + 8 * k : 32 * b + 8 * k + 8] for k in range(4)]
        top = jnp.concatenate(rows[:2], axis=1)
        bottom = jnp.concatenate(rows[2:], axis=1)
        own = jnp.where(upper, top, bottom).astype(BF16)
        away = jnp.where(upper, bottom, top).astype(BF16)
        fields.append((own, away))
        passed = nt(own, chalf[b, pl.ds(mine, r), :]) + nt(away, ohalf[b, pl.ds(mine, r), :])
        give[b] = passed.astype(BF16)
        given.append(passed)

    po_copy = copy(give, po, po_send, po_recv, partner, partner_lat)
    start_copy = copy(
        give, cin, t_send, c_recv, layer - 3 * step, lat if groups == 2 else twin
    )
    q_copy = copy(qout, qin, q_send, q_recv, onward, next_lat)
    far_lat = jnp.where(place == groups - 3, twin, lat)
    c_copies = [
        copy(fout, cin, c_send.at[0], c_recv, onward, twin),
        copy(fout, cin, c_send.at[1], c_recv, layer + 4 * step, far_lat),
    ]
    o_copy = copy(fout, oin, o_send, o_recv, layer + step, jnp.where(odd, twin, lat))
    own_copy = copy(qout, osib, own_send, own_recv, layer, twin)
    both_copy = copy(fout, tin, c_send.at[2], trace_recv, onward, lat)
    hand_copy = copy(comp, usib, u_send, u_recv, layer, twin)
    twin_copy = copy(tout, oin, trace_send, o_recv, layer + step, twin)
    trace_copy = copy(tout, tin, trace_send, trace_recv, layer, twin)

    @pl.when(last)
    def _():
        start_copy.start()

    po_copy.start()

    for b in range(blocks):
        own, away = fields[b]
        owned = nt(own, chalf[b, pl.ds(other, r), :]) + nt(away, ohalf[b, pl.ds(other, r), :])
        base[b] = owned
        qout[b] = owned.astype(BF16)

    @pl.when(first)
    def _():
        q_copy.start()

    @pl.when(odd & jnp.logical_not(last))
    def _():
        own_copy.start()

    for b in range(blocks):
        acc[b] = jnp.where(
            upper,
            jnp.concatenate([given[b], base[b]], axis=1),
            jnp.concatenate([base[b], given[b]], axis=1),
        )

    def opposite():
        o_copy.wait_recv()
        for b in range(blocks):
            acc[b] = acc[b] + nt(oin[b], ohalf[b])

    @pl.when(first)
    def _():
        po_copy.wait_recv()
        for b in range(blocks):
            fout[b] = (nt(po[b], step_of(b)) + base[b]).astype(BF16)
        o_copy.start()
        for b in range(blocks):
            acc[b] = acc[b] + nt(po[b], chalf[b])
        opposite()

    @pl.when(middle)
    def _():
        @pl.when(x == 1)
        def _():
            for i in range(2):
                compose(i)

        for i in range(2, len(parts_of)):
            compose(i)

        @pl.when(jnp.logical_not(upper_core))
        def _():
            hand_copy.start()

        po_copy.wait_recv()
        for b in range(blocks):
            total = nt(po[b], step_of(b)) + base[b]
            base[b] = total
            qout[b] = total.astype(BF16)
        q_copy.start()

        @pl.when(jnp.logical_not(upper_core))
        def _():
            own_copy.start()
            c_copies[0].wait_recv()

        @pl.when(upper_core)
        def _():
            hand_copy.wait_recv()
            own_copy.wait_recv()
            both_copy.wait_recv()
            for b in range(blocks):
                tout[b] = (nt(tin[b], usib[b]) + osib[b].astype(F32)).astype(BF16)
            twin_copy.start()
            c_copies[0].wait_recv()
            for b in range(blocks):
                fout[b] = (nt(cin[b], comp[b]) + base[b]).astype(BF16)
            o_copy.start()

        for b in range(blocks):
            trace = nt(cin[b], far[b]) + po[b].astype(F32)
            acc[b] = acc[b] + nt(trace.astype(BF16), chalf[b])
        opposite()

    def steps():
        for i in range(sent):
            comp_copies[i].wait_recv()

        @pl.when(place == 1)
        def _():
            for i in range(sent, len(parts_of)):
                comp_copies[i].wait_recv()

        @pl.when(place > 1)
        def _():
            head_copy.wait_recv()
            tail_copy.wait_recv()
            zfar[0, :, end] = jnp.dot(
                head[...], tail[...], preferred_element_type=F32
            ).astype(BF16)

    @pl.when(last)
    def _():
        for far_copy in far_copies:
            far_copy.wait_recv()
        steps()
        for b in range(blocks):
            comp[b] = jnp.dot(far[b], zfar[b], preferred_element_type=F32).astype(BF16)
        po_copy.wait_recv()
        q_copy.wait_recv()
        rest = []
        for b in range(blocks):
            part = nt(qin[b], far[b]) + po[b].astype(F32)
            rest.append(part)
        c_copies[0].wait_recv()
        for b in range(blocks):
            trace = nt(cin[b], comp[b]) + rest[b]
            acc[b] = acc[b] + nt(trace.astype(BF16), chalf[b])

    @pl.when(odd & jnp.logical_not(last))
    def _():
        u_copy.wait_recv()
        for i, (b, h) in enumerate(parts_of):
            far_copies[i].wait_recv()
            comp[b, :, h] = jnp.dot(
                usib[b], far[b, :, h], preferred_element_type=F32
            ).astype(BF16)
        po_copy.wait_recv()
        own_copy.wait_recv()
        rest = [nt(po[b], usib[b]) + osib[b].astype(F32) for b in range(blocks)]
        steps()
        q_copy.wait_recv()
        c_copies[0].wait_recv()
        middles = []
        for b in range(blocks):
            between = (nt(cin[b], zfar[b]) + qin[b].astype(F32)).astype(BF16)
            fout[b] = (nt(between, comp[b]) + rest[b]).astype(BF16)
            middles.append(between)
        c_copies[1].start()

        @pl.when(upper_core)
        def _():
            both_copy.start()

        c_copies[0].start()
        o_copy.start()
        for b in range(blocks):
            tout[b] = (nt(middles[b], far[b]) + po[b].astype(F32)).astype(BF16)
        trace_copy.start()
        trace_copy.wait_recv()
        for b in range(blocks):
            acc[b] = acc[b] + nt(tin[b], chalf[b])
        opposite()

    for b in range(blocks):
        out[0, b] = acc[b]

    @pl.when(jnp.logical_not(last))
    def _():
        for far_copy in far_copies:
            far_copy.wait_send()

    @pl.when(last)
    def _():
        start_copy.wait_send()

    @pl.when(first)
    def _():
        for comp_copy in comp_copies[sent:]:
            comp_copy.wait_send()

    @pl.when(middle)
    def _():
        head_copy.wait_send()

        @pl.when(upper_core)
        def _():
            twin_copy.wait_send()

        @pl.when(jnp.logical_not(upper_core))
        def _():
            hand_copy.wait_send()
            own_copy.wait_send()

    @pl.when(odd & jnp.logical_not(last) & upper_core)
    def _():
        both_copy.wait_send()

    @pl.when(jnp.logical_not(last | (middle & jnp.logical_not(upper_core))))
    def _():
        o_copy.wait_send()

    @pl.when(jnp.logical_not(odd))
    def _():
        for comp_copy in comp_copies[:sent]:
            comp_copy.wait_send()
        q_copy.wait_send()

    @pl.when(odd & jnp.logical_not(last))
    def _():
        for c_copy in [*c_copies, u_copy, own_copy, trace_copy, tail_copy]:
            c_copy.wait_send()

    po_copy.wait_send()
    pltpu.make_async_copy(send.at[everyone], send.at[everyone], send_sem).wait()


def body(layers, lateral, inverse, tiles, tile_dest, tile_code):
    devices = layers * lateral
    _, blocks, size, _ = inverse.shape
    r = tiles.shape[1]
    src = 8
    dma = pltpu.SemaphoreType.DMA
    small = (blocks, src, r)
    matrix = pltpu.VMEM((blocks, r, r), BF16)
    vmem = pl.BlockSpec(memory_space=pltpu.VMEM)
    return pl.pallas_call(
        functools.partial(kernel, layers, lateral),
        out_shape=jax.ShapeDtypeStruct((1, blocks, src, size), F32),
        in_specs=[pl.BlockSpec(memory_space=pltpu.HBM)] * 4,
        out_specs=vmem,
        scratch_shapes=[
            pltpu.VMEM(tiles.shape, BF16),
            pltpu.VMEM((1, tiles.shape[0]), jnp.int32),
            pltpu.VMEM((1, tiles.shape[0]), jnp.int32),
            pltpu.VMEM((devices, 8, r // 2), BF16),
            pltpu.VMEM((devices, 8, r // 2), BF16),
            pltpu.VMEM((blocks, size, r), BF16),
            pltpu.VMEM((blocks, size, r), BF16),
            matrix, matrix, matrix,
            pltpu.VMEM((blocks, src, size), F32),
            pltpu.VMEM(small, F32),
        ]
        + [pltpu.VMEM(small, BF16)] * 7
        + [matrix]
        + [pltpu.VMEM(small, BF16)] * 3
        + [pltpu.VMEM((r, r), BF16), pltpu.VMEM((r, r // 2), BF16)]
        + [dma((3,)), dma((2,)), dma, dma((2,))]
        + [dma((2 * blocks,))] * 4
        + [dma] * 3
        + [dma((3,))]
        + [dma] * 15,
        compiler_params=pltpu.CompilerParams(
            collective_id=0, has_side_effects=True, vmem_limit_bytes=48 * 1024 * 1024
        ),
        name="sweep",
    )(
        *(
            pltpu.with_memory_space_constraint(array, pltpu.HBM)
            for array in (inverse, tiles, tile_dest.reshape(1, -1), tile_code.reshape(1, -1))
        )
    )


def solution(mesh):
    in_specs = (
        P("layer", "lat", None, None),
        P(("layer", "lat"), None),
        P(("layer", "lat"), None),
        P(("layer", "lat")),
    )
    out_specs = P("layer", "lat", None, None)
    return jax.shard_map(
        functools.partial(body, mesh.shape["layer"], mesh.shape["lat"]),
        mesh=mesh, in_specs=in_specs, out_specs=out_specs, check_vma=False,
    )
```

```python
import functools

import jax
import jax.numpy as jnp
from jax import lax
from jax.experimental import pallas as pl
from jax.experimental.pallas import tpu as pltpu
from jax.sharding import PartitionSpec as P

MESH = pl.DeviceIdType.MESH
F32 = jnp.float32
BF16 = jnp.bfloat16
GROUP = 32
BATCH = 16


def nt(vectors, matrix):
    return lax.dot_general(vectors, matrix, (((1,), (1,)), ((), ())), preferred_element_type=F32)


def kernel(
    layers, lateral,
    inv, tiles_in, dest_in, code_in, out,
    tiles, dest, code, send, recv, chalf, ohalf, far, zfar, comp, acc, base, give, po, cin, oin, qin, qout, fout, usib, osib, tout, tin, head, tail,
    small_sem, load_sem, send_sem, recv_sem, far_send, far_recv, zfar_send, zfar_recv,
    po_send, po_recv, t_send, c_send, c_recv, o_send, o_recv, q_send, q_recv,
    head_send, head_recv, tail_send, tail_recv, u_send, u_recv, own_send, own_recv, trace_send, trace_recv,
):
    layer = lax.axis_index("layer")
    lat = lax.axis_index("lat")
    devices = layers * lateral
    me = layer * lateral + lat
    x = lax.rem(layer, 2)
    group = layer // 2
    groups = layers // 2
    step = 2 * x - 1
    place = jnp.where(x == 1, group, groups - 1 - group)
    blocks, size, r = chalf.shape
    count = tiles.shape[0]
    mine = pl.multiple_of((1 - x) * r, r)
    other = pl.multiple_of(x * r, r)
    first = place == 0
    last = place == groups - 1
    odd = lax.rem(place, 2) == 1
    middle = jnp.logical_not(odd | first)
    twin = lat + 1 - 2 * lax.rem(lat, 2)
    partner_lat = jnp.where(middle, twin, lat)
    upper_core = lax.rem(lat, 2) == 1
    next_lat = jnp.where(place == groups - 2, lat, twin)

    def others(visit, pick, begin, end):
        def visit_layer(i):
            to = pick(i)

            for across in range(1, lateral):
                visit(to, wrap(lat + across, lateral))

            @pl.when(to != layer)
            def _():
                visit(to, lat)

        if devices == GROUP:
            for i in range(begin, end):
                visit_layer(i)
        else:
            pl.loop(begin, end)(visit_layer)

    def wrap(index, length):
        return jnp.where(index >= length, index - length, index)

    smalls = [
        pltpu.make_async_copy(source, target, small_sem.at[i])
        for i, (source, target) in enumerate(((tiles_in, tiles), (dest_in, dest), (code_in, code)))
    ]
    for load in smalls:
        load.start()
    loads = [
        pltpu.make_async_copy(inv.at[0, :, :, pl.ds(mine, r)], chalf, load_sem.at[0]),
        pltpu.make_async_copy(inv.at[0, :, :, pl.ds(other, r)], ohalf, load_sem.at[1]),
    ]
    for load in loads:
        load.start()

    barrier = pltpu.get_barrier_semaphore()

    def greet(to_layer, to_lat):
        pl.semaphore_signal(
            barrier, inc=1, device_id=(to_layer, to_lat), device_id_type=MESH
        )

    others(greet, lambda i: i, 0, layers)

    for load in smalls:
        load.wait()

    row_t = lax.broadcasted_iota(jnp.int32, (count, count), 0)
    col_t = lax.broadcasted_iota(jnp.int32, (count, count), 1)
    target = dest[...]
    across = jnp.broadcast_to(target, (count, count))
    named = jnp.sum(jnp.where(row_t == col_t, across, 0), axis=1, keepdims=True)
    order = jnp.sum(
        jnp.where((named == target) & (row_t < col_t), 1, 0), axis=0, keepdims=True
    )
    codes = jnp.broadcast_to(code[...], (count, count)) + 1
    code_col = jnp.sum(jnp.where(row_t == col_t, codes, 0), axis=1, keepdims=True)
    half = r // 2
    parts = [
        tiles[:, :half],
        tiles[:, half:],
        jnp.broadcast_to(code_col, (count, half)).astype(F32).astype(BF16),
    ]
    shape_w = (GROUP * 8, count)
    row_w = lax.broadcasted_iota(jnp.int32, shape_w, 0)
    q_w = row_w % 8
    slot_w = jnp.where(q_w < 4, q_w // 2, q_w - 4)
    kind_w = jnp.where(q_w < 4, q_w % 2, jnp.where(q_w < 6, 2, 3))

    def pack(chunk):
        hit = (target == chunk * GROUP + row_w // 8) & (order == slot_w)
        message = jnp.zeros((GROUP * 8, half), F32)
        for kind, part in enumerate(parts):
            picks = jnp.where(hit & (kind_w == kind), 1.0, 0.0).astype(BF16)
            message = message + jnp.dot(picks, part, preferred_element_type=F32)
        send[pl.ds(chunk * GROUP, GROUP)] = message.reshape(GROUP, 8, half).astype(BF16)

    if devices == GROUP:
        pack(0)
    else:
        pl.loop(0, devices // GROUP)(pack)
    recv[me] = send[me]

    pl.semaphore_wait(barrier, devices - 1)

    side = layer // groups
    side_size = devices // 2

    def route(to_layer, to_lat):
        pltpu.make_async_remote_copy(
            src_ref=send.at[to_layer * lateral + to_lat],
            dst_ref=recv.at[me],
            send_sem=send_sem,
            recv_sem=recv_sem.at[side],
            device_id=(to_layer, to_lat),
            device_id_type=MESH,
        ).start()

    def copy(source, target, send_at, recv_at, to, to_lat):
        return pltpu.make_async_remote_copy(
            src_ref=source, dst_ref=target, send_sem=send_at, recv_sem=recv_at,
            device_id=(to, to_lat), device_id_type=MESH,
        )

    partner = layer - step
    onward = layer + 2 * step
    parts_of = [(b, pl.ds(h, half)) for b in reversed(range(blocks)) for h in range(0, r, half)]
    sent = len(parts_of) - 1
    far_copies = [
        copy(
            inv.at[0, b, pl.ds(mine, r), pl.ds(pl.multiple_of(other + h.start, half), half)],
            far.at[b, :, h], far_send.at[i], far_recv.at[i], partner, partner_lat,
        )
        for i, (b, h) in enumerate(parts_of)
    ]
    raw_copies = [
        copy(
            inv.at[0, b, pl.ds(other, r), pl.ds(pl.multiple_of(mine + h.start, half), half)],
            zfar.at[b, :, h], zfar_send.at[i], zfar_recv.at[i], onward, next_lat,
        )
        for i, (b, h) in enumerate(parts_of)
    ]
    comp_copies = [
        copy(
            comp.at[b, :, h], zfar.at[b, :, h],
            zfar_send.at[i], zfar_recv.at[i], onward, next_lat,
        )
        for i, (b, h) in enumerate(parts_of)
    ]

    end = parts_of[-1][1]
    head_copy = copy(
        inv.at[0, 0, pl.ds(other, r), pl.ds(mine, r)], head, head_send, head_recv, onward, next_lat
    )
    tail_copy = copy(
        inv.at[0, 0, pl.ds(mine, r), pl.ds(pl.multiple_of(other + end.start, half), half)],
        tail, tail_send, tail_recv,
        layer - 3 * step, jnp.where(place == 1, lat, twin),
    )

    turned = first & (x == 0)

    @pl.when(jnp.logical_not(turned))
    def _():
        for across in range(lateral):
            route(partner, wrap(lat + across, lateral))

    @pl.when(jnp.where(first, x == 1, jnp.logical_not(last)))
    def _():
        for far_copy in far_copies[:sent]:
            far_copy.start()

    @pl.when(jnp.where(first, x == 1, middle))
    def _():
        for far_copy in far_copies[sent:]:
            far_copy.start()

    def route_far(to_layer, to_lat):
        @pl.when(turned | (to_layer != partner))
        def _():
            route(to_layer, to_lat)

    def downward(i):
        at = jnp.where(turned, layers - 3, layers - 1) - i
        return jnp.where(at < 0, at + layers, at)

    others(route_far, downward, 0, layers - 2)

    @pl.when(first)
    def _():
        for raw_copy in raw_copies:
            raw_copy.start()

    others(route_far, downward, layers - 2, layers)

    @pl.when(middle)
    def _():
        head_copy.start()

    @pl.when(odd & jnp.logical_not(last))
    def _():
        tail_copy.start()

    @pl.when(turned)
    def _():
        for far_copy in far_copies:
            far_copy.start()

    for load in loads:
        load.wait()

    u_copy = copy(
        chalf.at[:, pl.ds(other, r), :], usib, u_send, u_recv, layer, twin
    )

    @pl.when(odd & jnp.logical_not(last))
    def _():
        u_copy.start()

    def step_of(b):
        return chalf[b, pl.ds(other, r), :]

    def compose(i):
        b, h = parts_of[i]
        far_copies[i].wait_recv()
        comp[b, :, h] = jnp.dot(
            step_of(b), far[b, :, h], preferred_element_type=F32
        ).astype(BF16)
        if i < sent:
            comp_copies[i].start()

    @pl.when(middle & (x == 0))
    def _():
        for i in range(2):
            compose(i)

    everyone = pl.ds(0, devices - 1)

    shape_u = (BATCH, 8, half)
    q_u = lax.broadcasted_iota(jnp.int32, shape_u, 1)
    lane = lax.broadcasted_iota(jnp.int32, shape_u, 2)
    s_of, half_of, plane_of, block_of = lane % 8, (lane // 8) % 2, (lane // 16) % 2, lane // 32
    wanted = (((s_of * 2 + plane_of) * blocks + block_of) + 1).astype(F32)
    usable = (q_u < 4) & (q_u % 2 == half_of) & (lane < 64)

    def unpack(begin):
        got = recv[pl.ds(begin, BATCH)].astype(F32)
        named_code = jnp.where(q_u < 2, got[:, 4:5, :], got[:, 5:6, :])
        table = jnp.where(usable & (named_code == wanted), 1.0, 0.0)
        return lax.dot_general(
            table.reshape(BATCH * 8, half).astype(BF16),
            got.reshape(BATCH * 8, half).astype(BF16),
            (((0,), (0,)), ((), ())),
            preferred_element_type=F32,
        )

    def unpack_side(at):
        begin = at * side_size
        if side_size == BATCH:
            return unpack(begin)
        return lax.fori_loop(
            0, side_size // BATCH, lambda i, total: total + unpack(begin + i * BATCH),
            jnp.zeros((half, half), F32),
        )

    near = recv.at[pl.ds(0, side_size - 1)]
    distant = recv.at[pl.ds(0, side_size)]
    pltpu.make_async_copy(near, near, recv_sem.at[side]).wait()
    field = unpack_side(side)
    pltpu.make_async_copy(distant, distant, recv_sem.at[1 - side]).wait()
    field = field + unpack_side(1 - side)

    upper = x == 1
    fields, given = [], []
    for b in range(blocks):
        rows = [field[32 * b + 8 * k : 32 * b + 8 * k + 8] for k in range(4)]
        top = jnp.concatenate(rows[:2], axis=1)
        bottom = jnp.concatenate(rows[2:], axis=1)
        own = jnp.where(upper, top, bottom).astype(BF16)
        away = jnp.where(upper, bottom, top).astype(BF16)
        fields.append((own, away))
        passed = nt(own, chalf[b, pl.ds(mine, r), :]) + nt(away, ohalf[b, pl.ds(mine, r), :])
        give[b] = passed.astype(BF16)
        given.append(passed)

    po_copy = copy(give, po, po_send, po_recv, partner, partner_lat)
    start_copy = copy(
        give, cin, t_send, c_recv, layer - 3 * step, lat if groups == 2 else twin
    )
    q_copy = copy(qout, qin, q_send, q_recv, onward, next_lat)
    far_lat = jnp.where(place == groups - 3, twin, lat)
    c_copies = [
        copy(fout, cin, c_send.at[0], c_recv, onward, twin),
        copy(fout, cin, c_send.at[1], c_recv, layer + 4 * step, far_lat),
    ]
    o_copy = copy(fout, oin, o_send, o_recv, layer + step, jnp.where(odd, twin, lat))
    own_copy = copy(qout, osib, own_send, own_recv, layer, twin)
    both_copy = copy(fout, tin, c_send.at[2], trace_recv, onward, lat)
    hand_copy = copy(comp, usib, u_send, u_recv, layer, twin)
    twin_copy = copy(tout, oin, trace_send, o_recv, layer + step, twin)
    trace_copy = copy(tout, tin, trace_send, trace_recv, layer, twin)

    @pl.when(last)
    def _():
        start_copy.start()

    po_copy.start()

    @pl.when(odd & jnp.logical_not(last))
    def _():
        for far_copy in far_copies[sent:]:
            far_copy.start()

    for b in range(blocks):
        own, away = fields[b]
        owned = nt(own, chalf[b, pl.ds(other, r), :]) + nt(away, ohalf[b, pl.ds(other, r), :])
        base[b] = owned
        qout[b] = owned.astype(BF16)

    @pl.when(first)
    def _():
        q_copy.start()

    @pl.when(odd & jnp.logical_not(last))
    def _():
        own_copy.start()

    for b in range(blocks):
        acc[b] = jnp.where(
            upper,
            jnp.concatenate([given[b], base[b]], axis=1),
            jnp.concatenate([base[b], given[b]], axis=1),
        )

    def opposite():
        o_copy.wait_recv()
        for b in range(blocks):
            acc[b] = acc[b] + nt(oin[b], ohalf[b])

    @pl.when(first)
    def _():
        po_copy.wait_recv()
        for b in range(blocks):
            fout[b] = (nt(po[b], step_of(b)) + base[b]).astype(BF16)
        o_copy.start()
        for b in range(blocks):
            acc[b] = acc[b] + nt(po[b], chalf[b])
        opposite()

    @pl.when(middle)
    def _():
        @pl.when(x == 1)
        def _():
            for i in range(2):
                compose(i)

        compose(2)
        po_copy.wait_recv()
        for b in range(blocks):
            total = nt(po[b], step_of(b)) + base[b]
            base[b] = total
            qout[b] = total.astype(BF16)
        q_copy.start()
        for i in range(3, len(parts_of)):
            compose(i)

        @pl.when(jnp.logical_not(upper_core))
        def _():
            hand_copy.start()

        @pl.when(jnp.logical_not(upper_core))
        def _():
            own_copy.start()
            c_copies[0].wait_recv()

        @pl.when(upper_core)
        def _():
            hand_copy.wait_recv()
            own_copy.wait_recv()
            both_copy.wait_recv()
            for b in range(blocks):
                tout[b] = (nt(tin[b], usib[b]) + osib[b].astype(F32)).astype(BF16)
            twin_copy.start()
            c_copies[0].wait_recv()
            for b in range(blocks):
                fout[b] = (nt(cin[b], comp[b]) + base[b]).astype(BF16)
            o_copy.start()

        for b in range(blocks):
            trace = nt(cin[b], far[b]) + po[b].astype(F32)
            acc[b] = acc[b] + nt(trace.astype(BF16), chalf[b])
        opposite()

    def steps():
        for i in range(sent):
            comp_copies[i].wait_recv()

        @pl.when(place == 1)
        def _():
            for i in range(sent, len(parts_of)):
                comp_copies[i].wait_recv()

        @pl.when(place > 1)
        def _():
            head_copy.wait_recv()
            tail_copy.wait_recv()
            zfar[0, :, end] = jnp.dot(
                head[...], tail[...], preferred_element_type=F32
            ).astype(BF16)

    @pl.when(last)
    def _():
        for far_copy in far_copies:
            far_copy.wait_recv()
        steps()
        for b in range(blocks):
            comp[b] = jnp.dot(far[b], zfar[b], preferred_element_type=F32).astype(BF16)
        po_copy.wait_recv()
        q_copy.wait_recv()
        rest = []
        for b in range(blocks):
            part = nt(qin[b], far[b]) + po[b].astype(F32)
            rest.append(part)
        c_copies[0].wait_recv()
        for b in range(blocks):
            trace = nt(cin[b], comp[b]) + rest[b]
            acc[b] = acc[b] + nt(trace.astype(BF16), chalf[b])

    @pl.when(odd & jnp.logical_not(last))
    def _():
        u_copy.wait_recv()
        for i, (b, h) in enumerate(parts_of):
            far_copies[i].wait_recv()
            comp[b, :, h] = jnp.dot(
                usib[b], far[b, :, h], preferred_element_type=F32
            ).astype(BF16)
        po_copy.wait_recv()
        own_copy.wait_recv()
        rest = [nt(po[b], usib[b]) + osib[b].astype(F32) for b in range(blocks)]
        steps()
        q_copy.wait_recv()
        c_copies[0].wait_recv()
        middles = []
        for b in range(blocks):
            between = (nt(cin[b], zfar[b]) + qin[b].astype(F32)).astype(BF16)
            fout[b] = (nt(between, comp[b]) + rest[b]).astype(BF16)
            middles.append(between)
        c_copies[1].start()

        @pl.when(upper_core)
        def _():
            both_copy.start()

        c_copies[0].start()
        o_copy.start()
        for b in range(blocks):
            tout[b] = (nt(middles[b], far[b]) + po[b].astype(F32)).astype(BF16)
        trace_copy.start()
        trace_copy.wait_recv()
        for b in range(blocks):
            acc[b] = acc[b] + nt(tin[b], chalf[b])
        opposite()

    for b in range(blocks):
        out[0, b] = acc[b]

    @pl.when(jnp.logical_not(last))
    def _():
        for far_copy in far_copies:
            far_copy.wait_send()

    @pl.when(last)
    def _():
        start_copy.wait_send()

    @pl.when(first)
    def _():
        for comp_copy in comp_copies[sent:]:
            comp_copy.wait_send()

    @pl.when(middle)
    def _():
        head_copy.wait_send()

        @pl.when(upper_core)
        def _():
            twin_copy.wait_send()

        @pl.when(jnp.logical_not(upper_core))
        def _():
            hand_copy.wait_send()
            own_copy.wait_send()

    @pl.when(odd & jnp.logical_not(last) & upper_core)
    def _():
        both_copy.wait_send()

    @pl.when(jnp.logical_not(last | (middle & jnp.logical_not(upper_core))))
    def _():
        o_copy.wait_send()

    @pl.when(jnp.logical_not(odd))
    def _():
        for comp_copy in comp_copies[:sent]:
            comp_copy.wait_send()
        q_copy.wait_send()

    @pl.when(odd & jnp.logical_not(last))
    def _():
        for c_copy in [*c_copies, u_copy, own_copy, trace_copy, tail_copy]:
            c_copy.wait_send()

    po_copy.wait_send()
    pltpu.make_async_copy(send.at[everyone], send.at[everyone], send_sem).wait()


def body(layers, lateral, inverse, tiles, tile_dest, tile_code):
    devices = layers * lateral
    _, blocks, size, _ = inverse.shape
    r = tiles.shape[1]
    src = 8
    dma = pltpu.SemaphoreType.DMA
    small = (blocks, src, r)
    matrix = pltpu.VMEM((blocks, r, r), BF16)
    vmem = pl.BlockSpec(memory_space=pltpu.VMEM)
    return pl.pallas_call(
        functools.partial(kernel, layers, lateral),
        out_shape=jax.ShapeDtypeStruct((1, blocks, src, size), F32),
        in_specs=[pl.BlockSpec(memory_space=pltpu.HBM)] * 4,
        out_specs=vmem,
        scratch_shapes=[
            pltpu.VMEM(tiles.shape, BF16),
            pltpu.VMEM((1, tiles.shape[0]), jnp.int32),
            pltpu.VMEM((1, tiles.shape[0]), jnp.int32),
            pltpu.VMEM((devices, 8, r // 2), BF16),
            pltpu.VMEM((devices, 8, r // 2), BF16),
            pltpu.VMEM((blocks, size, r), BF16),
            pltpu.VMEM((blocks, size, r), BF16),
            matrix, matrix, matrix,
            pltpu.VMEM((blocks, src, size), F32),
            pltpu.VMEM(small, F32),
        ]
        + [pltpu.VMEM(small, BF16)] * 7
        + [matrix]
        + [pltpu.VMEM(small, BF16)] * 3
        + [pltpu.VMEM((r, r), BF16), pltpu.VMEM((r, r // 2), BF16)]
        + [dma((3,)), dma((2,)), dma, dma((2,))]
        + [dma((2 * blocks,))] * 4
        + [dma] * 3
        + [dma((3,))]
        + [dma] * 15,
        compiler_params=pltpu.CompilerParams(
            collective_id=0, has_side_effects=True, vmem_limit_bytes=48 * 1024 * 1024
        ),
        name="sweep",
    )(
        *(
            pltpu.with_memory_space_constraint(array, pltpu.HBM)
            for array in (inverse, tiles, tile_dest.reshape(1, -1), tile_code.reshape(1, -1))
        )
    )


def solution(mesh):
    in_specs = (
        P("layer", "lat", None, None),
        P(("layer", "lat"), None),
        P(("layer", "lat"), None),
        P(("layer", "lat")),
    )
    out_specs = P("layer", "lat", None, None)
    return jax.shard_map(
        functools.partial(body, mesh.shape["layer"], mesh.shape["lat"]),
        mesh=mesh, in_specs=in_specs, out_specs=out_specs, check_vma=False,
    )
```

```python
import functools

import jax
import jax.numpy as jnp
from jax import lax
from jax.experimental import pallas as pl
from jax.experimental.pallas import tpu as pltpu
from jax.sharding import PartitionSpec as P

MESH = pl.DeviceIdType.MESH
F32 = jnp.float32
BF16 = jnp.bfloat16
GROUP = 32
BATCH = 16


def nt(vectors, matrix):
    return lax.dot_general(vectors, matrix, (((1,), (1,)), ((), ())), preferred_element_type=F32)


def kernel(
    layers, lateral,
    inv, tiles_in, dest_in, code_in, out, extra,
    tiles, dest, code, send, recv, chalf, ohalf, far, zfar, comp, base, give, po, cin, oin, qin, qout, fout, usib, osib, tout, tin, head, tail,
    small_sem, load_sem, send_sem, recv_sem, far_send, far_recv, zfar_send, zfar_recv,
    po_send, po_recv, t_send, c_send, c_recv, o_send, o_recv, q_send, q_recv,
    head_send, head_recv, tail_send, tail_recv, u_send, u_recv, own_send, own_recv, trace_send, trace_recv,
):
    layer = lax.axis_index("layer")
    lat = lax.axis_index("lat")
    devices = layers * lateral
    me = layer * lateral + lat
    x = lax.rem(layer, 2)
    group = layer // 2
    groups = layers // 2
    step = 2 * x - 1
    place = jnp.where(x == 1, group, groups - 1 - group)
    blocks, size, r = chalf.shape
    acc = out.at[0]
    count = tiles.shape[0]
    mine = pl.multiple_of((1 - x) * r, r)
    other = pl.multiple_of(x * r, r)
    first = place == 0
    last = place == groups - 1
    odd = lax.rem(place, 2) == 1
    middle = jnp.logical_not(odd | first)
    twin = lat + 1 - 2 * lax.rem(lat, 2)
    partner_lat = jnp.where(middle, twin, lat)
    upper_core = lax.rem(lat, 2) == 1
    next_lat = jnp.where(place == groups - 2, lat, twin)

    def others(visit, pick, begin, end):
        def visit_layer(i):
            to = pick(i)

            @pl.when(to != layer)
            def _():
                visit(to, lat)

            for across in [*range(2, lateral, 2), *range(1, lateral, 2)]:
                visit(to, wrap(lat + across, lateral))

        if devices == GROUP:
            for i in range(begin, end):
                visit_layer(i)
        else:
            pl.loop(begin, end)(visit_layer)

    def wrap(index, length):
        return jnp.where(index >= length, index - length, index)

    smalls = [
        pltpu.make_async_copy(source, target, small_sem.at[i])
        for i, (source, target) in enumerate(((tiles_in, tiles), (dest_in, dest), (code_in, code)))
    ]
    barrier = pltpu.get_barrier_semaphore()

    def greet(to_layer, to_lat):
        pl.semaphore_signal(
            barrier, inc=1, device_id=(to_layer, to_lat), device_id_type=MESH
        )

    others(greet, lambda i: i, 0, 2)

    for load in smalls:
        load.start()
    loads = [
        pltpu.make_async_copy(inv.at[0, :, :, pl.ds(mine, r)], chalf, load_sem.at[0]),
        pltpu.make_async_copy(inv.at[0, :, :, pl.ds(other, r)], ohalf, load_sem.at[1]),
    ]
    for load in loads:
        load.start()

    others(greet, lambda i: i, 2, layers)

    for load in smalls:
        load.wait()

    row_t = lax.broadcasted_iota(jnp.int32, (count, count), 0)
    col_t = lax.broadcasted_iota(jnp.int32, (count, count), 1)
    target = dest[...]
    across = jnp.broadcast_to(target, (count, count))
    named = jnp.sum(jnp.where(row_t == col_t, across, 0), axis=1, keepdims=True)
    order = jnp.sum(
        jnp.where((named == target) & (row_t < col_t), 1, 0), axis=0, keepdims=True
    )
    codes = jnp.broadcast_to(code[...], (count, count)) + 1
    code_col = jnp.sum(jnp.where(row_t == col_t, codes, 0), axis=1, keepdims=True)
    half = r // 2
    parts = [
        tiles[:, :half],
        tiles[:, half:],
        jnp.broadcast_to(code_col, (count, half)).astype(F32).astype(BF16),
    ]
    shape_w = (GROUP * 8, count)
    row_w = lax.broadcasted_iota(jnp.int32, shape_w, 0)
    q_w = row_w % 8
    slot_w = jnp.where(q_w < 4, q_w // 2, q_w - 4)
    kind_w = jnp.where(q_w < 4, q_w % 2, jnp.where(q_w < 6, 2, 3))

    def pack(chunk):
        hit = (target == chunk * GROUP + row_w // 8) & (order == slot_w)
        message = jnp.zeros((GROUP * 8, half), F32)
        for kind, part in enumerate(parts):
            picks = jnp.where(hit & (kind_w == kind), 1.0, 0.0).astype(BF16)
            message = message + jnp.dot(picks, part, preferred_element_type=F32)
        send[pl.ds(chunk * GROUP, GROUP)] = message.reshape(GROUP, 8, half).astype(BF16)

    if devices == GROUP:
        pack(0)
    else:
        pl.loop(0, devices // GROUP)(pack)
    recv[me] = send[me]

    pl.semaphore_wait(barrier, devices - 1)

    side = layer // groups
    side_size = devices // 2

    def route(to_layer, to_lat):
        pltpu.make_async_remote_copy(
            src_ref=send.at[to_layer * lateral + to_lat],
            dst_ref=recv.at[me],
            send_sem=send_sem,
            recv_sem=recv_sem.at[side],
            device_id=(to_layer, to_lat),
            device_id_type=MESH,
        ).start()

    def copy(source, target, send_at, recv_at, to, to_lat):
        return pltpu.make_async_remote_copy(
            src_ref=source, dst_ref=target, send_sem=send_at, recv_sem=recv_at,
            device_id=(to, to_lat), device_id_type=MESH,
        )

    partner = layer - step
    onward = layer + 2 * step
    parts_of = [(b, pl.ds(h, half)) for b in reversed(range(blocks)) for h in range(0, r, half)]
    sent = len(parts_of) - 1
    far_copies = [
        copy(
            inv.at[0, b, pl.ds(mine, r), pl.ds(pl.multiple_of(other + h.start, half), half)],
            far.at[b, :, h], far_send.at[i], far_recv.at[i], partner, partner_lat,
        )
        for i, (b, h) in enumerate(parts_of)
    ]
    raw_copies = [
        copy(
            inv.at[0, b, pl.ds(other, r), pl.ds(pl.multiple_of(mine + h.start, half), half)],
            zfar.at[b, :, h], zfar_send.at[i], zfar_recv.at[i], onward, next_lat,
        )
        for i, (b, h) in enumerate(parts_of)
    ]
    comp_copies = [
        copy(
            comp.at[b, :, h], zfar.at[b, :, h],
            zfar_send.at[i], zfar_recv.at[i], onward, next_lat,
        )
        for i, (b, h) in enumerate(parts_of)
    ]

    end = parts_of[-1][1]
    head_copy = copy(
        inv.at[0, 0, pl.ds(other, r), pl.ds(mine, r)], head, head_send, head_recv, onward, next_lat
    )
    tail_copy = copy(
        inv.at[0, 0, pl.ds(mine, r), pl.ds(pl.multiple_of(other + end.start, half), half)],
        tail, tail_send, tail_recv,
        layer - 3 * step, jnp.where(place == 1, lat, twin),
    )

    turned = first & (x == 0)

    @pl.when(jnp.logical_not(turned))
    def _():
        for across in range(lateral):
            route(partner, wrap(lat + across, lateral))

    @pl.when(jnp.where(first, x == 1, jnp.logical_not(last)))
    def _():
        for far_copy in far_copies[:sent]:
            far_copy.start()

    @pl.when(jnp.where(first, x == 1, middle))
    def _():
        for far_copy in far_copies[sent:]:
            far_copy.start()

    def route_far(to_layer, to_lat):
        @pl.when(turned | (to_layer != partner))
        def _():
            route(to_layer, to_lat)

    def downward(i):
        at = jnp.where(turned, layers - 3, layers - 1) - i
        return jnp.where(at < 0, at + layers, at)

    others(route_far, downward, 0, layers - 2)

    @pl.when(first)
    def _():
        for raw_copy in raw_copies:
            raw_copy.start()

    others(route_far, downward, layers - 2, layers)

    @pl.when(middle)
    def _():
        head_copy.start()

    @pl.when(odd & jnp.logical_not(last))
    def _():
        tail_copy.start()

    @pl.when(turned)
    def _():
        for far_copy in far_copies:
            far_copy.start()

    for load in loads:
        load.wait()

    u_copy = copy(
        chalf.at[:, pl.ds(other, r), :], usib, u_send, u_recv, layer, twin
    )

    @pl.when(odd & jnp.logical_not(last))
    def _():
        u_copy.start()

    def step_of(b):
        return chalf[b, pl.ds(other, r), :]

    def compose(i):
        b, h = parts_of[i]
        far_copies[i].wait_recv()
        comp[b, :, h] = jnp.dot(
            step_of(b), far[b, :, h], preferred_element_type=F32
        ).astype(BF16)
        if i < sent:
            comp_copies[i].start()

    @pl.when(middle & (x == 0))
    def _():
        for i in range(2):
            compose(i)

    everyone = pl.ds(0, devices - 1)

    shape_u = (BATCH, 8, half)
    q_u = lax.broadcasted_iota(jnp.int32, shape_u, 1)
    lane = lax.broadcasted_iota(jnp.int32, shape_u, 2)
    s_of, half_of, plane_of, block_of = lane % 8, (lane // 8) % 2, (lane // 16) % 2, lane // 32
    wanted = (((s_of * 2 + plane_of) * blocks + block_of) + 1).astype(F32)
    usable = (q_u < 4) & (q_u % 2 == half_of) & (lane < 64)

    def unpack(begin):
        got = recv[pl.ds(begin, BATCH)].astype(F32)
        named_code = jnp.where(q_u < 2, got[:, 4:5, :], got[:, 5:6, :])
        table = jnp.where(usable & (named_code == wanted), 1.0, 0.0)
        return lax.dot_general(
            table.reshape(BATCH * 8, half).astype(BF16),
            got.reshape(BATCH * 8, half).astype(BF16),
            (((0,), (0,)), ((), ())),
            preferred_element_type=F32,
        )

    def unpack_side(at):
        begin = at * side_size
        if side_size == BATCH:
            return unpack(begin)
        return lax.fori_loop(
            0, side_size // BATCH, lambda i, total: total + unpack(begin + i * BATCH),
            jnp.zeros((half, half), F32),
        )

    near = recv.at[pl.ds(0, side_size - 1)]
    distant = recv.at[pl.ds(0, side_size)]
    pltpu.make_async_copy(near, near, recv_sem.at[side]).wait()
    field = unpack_side(side)
    pltpu.make_async_copy(distant, distant, recv_sem.at[1 - side]).wait()
    field = field + unpack_side(1 - side)

    upper = x == 1
    fields, given = [], []
    for b in range(blocks):
        rows = [field[32 * b + 8 * k : 32 * b + 8 * k + 8] for k in range(4)]
        top = jnp.concatenate(rows[:2], axis=1)
        bottom = jnp.concatenate(rows[2:], axis=1)
        own = jnp.where(upper, top, bottom).astype(BF16)
        away = jnp.where(upper, bottom, top).astype(BF16)
        fields.append((own, away))
        passed = nt(own, chalf[b, pl.ds(mine, r), :]) + nt(away, ohalf[b, pl.ds(mine, r), :])
        give[b] = passed.astype(BF16)
        given.append(passed)

    po_copy = copy(give, po, po_send, po_recv, partner, partner_lat)
    start_copy = copy(
        give, cin, t_send, c_recv, layer - 3 * step, lat if groups == 2 else twin
    )
    q_copy = copy(qout, qin, q_send, q_recv, onward, next_lat)
    far_lat = jnp.where(place == groups - 3, twin, lat)
    c_copies = [
        copy(fout, cin, c_send.at[0], c_recv, onward, twin),
        copy(fout, cin, c_send.at[1], c_recv, layer + 4 * step, far_lat),
    ]
    o_copy = copy(fout, oin, o_send, o_recv, layer + step, jnp.where(odd, twin, lat))
    own_copy = copy(qout, osib, own_send, own_recv, layer, twin)
    both_copy = copy(fout, tin, c_send.at[2], trace_recv, onward, lat)
    hand_copy = copy(comp, usib, u_send, u_recv, layer, twin)
    twin_copy = copy(tout, oin, trace_send, o_recv, layer + step, twin)
    trace_copy = copy(tout, tin, trace_send, trace_recv, layer, twin)

    @pl.when(last)
    def _():
        start_copy.start()

    po_copy.start()

    @pl.when(odd & jnp.logical_not(last))
    def _():
        for far_copy in far_copies[sent:]:
            far_copy.start()

    for b in range(blocks):
        own, away = fields[b]
        owned = nt(own, chalf[b, pl.ds(other, r), :]) + nt(away, ohalf[b, pl.ds(other, r), :])
        base[b] = owned
        qout[b] = owned.astype(BF16)

    @pl.when(first)
    def _():
        q_copy.start()

    @pl.when(odd & jnp.logical_not(last))
    def _():
        own_copy.start()

    for b in range(blocks):
        acc[b] = jnp.where(
            upper,
            jnp.concatenate([given[b], base[b]], axis=1),
            jnp.concatenate([base[b], given[b]], axis=1),
        )

    def opposite():
        o_copy.wait_recv()
        for b in range(blocks):
            extra[0, b] = nt(oin[b], ohalf[b])

    @pl.when(first)
    def _():
        po_copy.wait_recv()
        for b in range(blocks):
            fout[b] = (nt(po[b], step_of(b)) + base[b]).astype(BF16)
        o_copy.start()
        for b in range(blocks):
            acc[b] = acc[b] + nt(po[b], chalf[b])
        opposite()

    @pl.when(middle)
    def _():
        @pl.when(x == 1)
        def _():
            for i in range(2):
                compose(i)

        compose(2)
        po_copy.wait_recv()
        for b in range(blocks):
            total = nt(po[b], step_of(b)) + base[b]
            base[b] = total
            qout[b] = total.astype(BF16)
        q_copy.start()
        for i in range(3, len(parts_of)):
            compose(i)

        @pl.when(jnp.logical_not(upper_core))
        def _():
            hand_copy.start()

        @pl.when(jnp.logical_not(upper_core))
        def _():
            own_copy.start()
            c_copies[0].wait_recv()

        @pl.when(upper_core)
        def _():
            hand_copy.wait_recv()
            own_copy.wait_recv()
            both_copy.wait_recv()
            for b in range(blocks):
                tout[b] = (nt(tin[b], usib[b]) + osib[b].astype(F32)).astype(BF16)
            twin_copy.start()
            c_copies[0].wait_recv()
            for b in range(blocks):
                fout[b] = (nt(cin[b], comp[b]) + base[b]).astype(BF16)
            o_copy.start()

        for b in range(blocks):
            trace = nt(cin[b], far[b]) + po[b].astype(F32)
            acc[b] = acc[b] + nt(trace.astype(BF16), chalf[b])
        opposite()

    def steps():
        for i in range(sent):
            comp_copies[i].wait_recv()

        @pl.when(place == 1)
        def _():
            for i in range(sent, len(parts_of)):
                comp_copies[i].wait_recv()

        @pl.when(place > 1)
        def _():
            head_copy.wait_recv()
            tail_copy.wait_recv()
            zfar[0, :, end] = jnp.dot(
                head[...], tail[...], preferred_element_type=F32
            ).astype(BF16)

    @pl.when(last)
    def _():
        for far_copy in far_copies:
            far_copy.wait_recv()
        steps()
        for b in range(blocks):
            comp[b] = jnp.dot(far[b], zfar[b], preferred_element_type=F32).astype(BF16)
        po_copy.wait_recv()
        q_copy.wait_recv()
        rest = []
        for b in range(blocks):
            part = nt(qin[b], far[b]) + po[b].astype(F32)
            rest.append(part)
        c_copies[0].wait_recv()
        for b in range(blocks):
            trace = nt(cin[b], comp[b]) + rest[b]
            extra[0, b] = nt(trace.astype(BF16), chalf[b])

    @pl.when(odd & jnp.logical_not(last))
    def _():
        u_copy.wait_recv()
        for i, (b, h) in enumerate(parts_of):
            far_copies[i].wait_recv()
            comp[b, :, h] = jnp.dot(
                usib[b], far[b, :, h], preferred_element_type=F32
            ).astype(BF16)
        po_copy.wait_recv()
        own_copy.wait_recv()
        rest = [nt(po[b], usib[b]) + osib[b].astype(F32) for b in range(blocks)]
        steps()
        q_copy.wait_recv()
        c_copies[0].wait_recv()
        middles = []
        for b in range(blocks):
            between = (nt(cin[b], zfar[b]) + qin[b].astype(F32)).astype(BF16)
            fout[b] = (nt(between, comp[b]) + rest[b]).astype(BF16)
            middles.append(between)
        @pl.when(upper_core)
        def _():
            c_copies[1].start()
            both_copy.start()
            c_copies[0].start()

        @pl.when(jnp.logical_not(upper_core))
        def _():
            c_copies[0].start()
            c_copies[1].start()

        o_copy.start()
        for b in range(blocks):
            tout[b] = (nt(middles[b], far[b]) + po[b].astype(F32)).astype(BF16)
        trace_copy.start()
        trace_copy.wait_recv()
        for b in range(blocks):
            acc[b] = acc[b] + nt(tin[b], chalf[b])
        opposite()

    @pl.when(jnp.logical_not(last))
    def _():
        for far_copy in far_copies:
            far_copy.wait_send()

    @pl.when(last)
    def _():
        start_copy.wait_send()

    @pl.when(first)
    def _():
        for comp_copy in comp_copies[sent:]:
            comp_copy.wait_send()

    @pl.when(middle)
    def _():
        head_copy.wait_send()

        @pl.when(upper_core)
        def _():
            twin_copy.wait_send()

        @pl.when(jnp.logical_not(upper_core))
        def _():
            hand_copy.wait_send()
            own_copy.wait_send()

    @pl.when(odd & jnp.logical_not(last) & upper_core)
    def _():
        both_copy.wait_send()

    @pl.when(jnp.logical_not(last | (middle & jnp.logical_not(upper_core))))
    def _():
        o_copy.wait_send()

    @pl.when(jnp.logical_not(odd))
    def _():
        for comp_copy in comp_copies[:sent]:
            comp_copy.wait_send()
        q_copy.wait_send()

    @pl.when(odd & jnp.logical_not(last))
    def _():
        for c_copy in [*c_copies, u_copy, own_copy, trace_copy, tail_copy]:
            c_copy.wait_send()

    po_copy.wait_send()
    pltpu.make_async_copy(send.at[everyone], send.at[everyone], send_sem).wait()


def body(layers, lateral, inverse, tiles, tile_dest, tile_code):
    devices = layers * lateral
    _, blocks, size, _ = inverse.shape
    r = tiles.shape[1]
    src = 8
    dma = pltpu.SemaphoreType.DMA
    small = (blocks, src, r)
    matrix = pltpu.VMEM((blocks, r, r), BF16)
    vmem = pl.BlockSpec(memory_space=pltpu.VMEM)
    most, final = pl.pallas_call(
        functools.partial(kernel, layers, lateral),
        out_shape=[jax.ShapeDtypeStruct((1, blocks, src, size), F32)] * 2,
        in_specs=[pl.BlockSpec(memory_space=pltpu.HBM)] * 4,
        out_specs=[vmem] * 2,
        scratch_shapes=[
            pltpu.VMEM(tiles.shape, BF16),
            pltpu.VMEM((1, tiles.shape[0]), jnp.int32),
            pltpu.VMEM((1, tiles.shape[0]), jnp.int32),
            pltpu.VMEM((devices, 8, r // 2), BF16),
            pltpu.VMEM((devices, 8, r // 2), BF16),
            pltpu.VMEM((blocks, size, r), BF16),
            pltpu.VMEM((blocks, size, r), BF16),
            matrix, matrix, matrix,
            pltpu.VMEM(small, F32),
        ]
        + [pltpu.VMEM(small, BF16)] * 7
        + [matrix]
        + [pltpu.VMEM(small, BF16)] * 3
        + [pltpu.VMEM((r, r), BF16), pltpu.VMEM((r, r // 2), BF16)]
        + [dma((3,)), dma((2,)), dma, dma((2,))]
        + [dma((2 * blocks,))] * 4
        + [dma] * 3
        + [dma((3,))]
        + [dma] * 15,
        compiler_params=pltpu.CompilerParams(
            collective_id=0, has_side_effects=True, vmem_limit_bytes=48 * 1024 * 1024
        ),
        name="sweep",
    )(
        *(
            pltpu.with_memory_space_constraint(array, pltpu.HBM)
            for array in (inverse, tiles, tile_dest.reshape(1, -1), tile_code.reshape(1, -1))
        )
    )
    return most + final


def solution(mesh):
    in_specs = (
        P("layer", "lat", None, None),
        P(("layer", "lat"), None),
        P(("layer", "lat"), None),
        P(("layer", "lat")),
    )
    out_specs = P("layer", "lat", None, None)
    return jax.shard_map(
        functools.partial(body, mesh.shape["layer"], mesh.shape["lat"]),
        mesh=mesh, in_specs=in_specs, out_specs=out_specs, check_vma=False,
    )
```

```python
import functools

import jax
import jax.numpy as jnp
from jax import lax
from jax.experimental import pallas as pl
from jax.experimental.pallas import tpu as pltpu
from jax.sharding import PartitionSpec as P

MESH = pl.DeviceIdType.MESH
F32 = jnp.float32
BF16 = jnp.bfloat16
GROUP = 32
BATCH = 16


def nt(vectors, matrix):
    return lax.dot_general(vectors, matrix, (((1,), (1,)), ((), ())), preferred_element_type=F32)


def kernel(
    layers, lateral,
    inv, tiles_in, dest_in, code_in, out, extra,
    tiles, dest, code, send, recv, chalf, ohalf, far, zfar, comp, base, give, po, cin, oin, qin, qout, fout, usib, osib, tout, tin, head, tail,
    small_sem, load_sem, send_sem, recv_sem, far_send, far_recv, zfar_send, zfar_recv,
    po_send, po_recv, t_send, c_send, c_recv, o_send, o_recv, q_send, q_recv,
    head_send, head_recv, tail_send, tail_recv, u_send, u_recv, own_send, own_recv, trace_send, trace_recv,
):
    layer = lax.axis_index("layer")
    lat = lax.axis_index("lat")
    devices = layers * lateral
    me = layer * lateral + lat
    x = lax.rem(layer, 2)
    group = layer // 2
    groups = layers // 2
    step = 2 * x - 1
    place = jnp.where(x == 1, group, groups - 1 - group)
    blocks, size, r = chalf.shape
    acc = out.at[0]
    count = tiles.shape[0]
    mine = pl.multiple_of((1 - x) * r, r)
    other = pl.multiple_of(x * r, r)
    first = place == 0
    last = place == groups - 1
    odd = lax.rem(place, 2) == 1
    middle = jnp.logical_not(odd | first)
    twin = lat + 1 - 2 * lax.rem(lat, 2)
    partner_lat = jnp.where(middle, twin, lat)
    upper_core = lax.rem(lat, 2) == 1
    next_lat = jnp.where(place == groups - 2, lat, twin)

    def others(visit, pick, begin, end):
        def visit_layer(i):
            to = pick(i)

            @pl.when(to != layer)
            def _():
                visit(to, lat)

            for across in [*range(2, lateral, 2), *range(1, lateral, 2)]:
                visit(to, wrap(lat + across, lateral))

        if devices == GROUP:
            for i in range(begin, end):
                visit_layer(i)
        else:
            pl.loop(begin, end)(visit_layer)

    def wrap(index, length):
        return jnp.where(index >= length, index - length, index)

    smalls = [
        pltpu.make_async_copy(source, target, small_sem.at[i])
        for i, (source, target) in enumerate(((tiles_in, tiles), (dest_in, dest), (code_in, code)))
    ]
    barrier = pltpu.get_barrier_semaphore()

    def greet(to_layer, to_lat):
        pl.semaphore_signal(
            barrier, inc=1, device_id=(to_layer, to_lat), device_id_type=MESH
        )

    others(greet, lambda i: i, 0, 2)

    for load in smalls:
        load.start()
    loads = [
        pltpu.make_async_copy(inv.at[0, :, :, pl.ds(mine, r)], chalf, load_sem.at[0]),
        pltpu.make_async_copy(inv.at[0, :, :, pl.ds(other, r)], ohalf, load_sem.at[1]),
    ]
    for load in loads:
        load.start()

    others(greet, lambda i: i, 2, layers)

    for load in smalls:
        load.wait()

    row_t = lax.broadcasted_iota(jnp.int32, (count, count), 0)
    col_t = lax.broadcasted_iota(jnp.int32, (count, count), 1)
    target = dest[...]
    across = jnp.broadcast_to(target, (count, count))
    named = jnp.sum(jnp.where(row_t == col_t, across, 0), axis=1, keepdims=True)
    order = jnp.sum(
        jnp.where((named == target) & (row_t < col_t), 1, 0), axis=0, keepdims=True
    )
    codes = jnp.broadcast_to(code[...], (count, count)) + 1
    code_col = jnp.sum(jnp.where(row_t == col_t, codes, 0), axis=1, keepdims=True)
    half = r // 2
    parts = [
        tiles[:, :half],
        tiles[:, half:],
        jnp.broadcast_to(code_col, (count, half)).astype(F32).astype(BF16),
    ]
    shape_w = (GROUP * 8, count)
    row_w = lax.broadcasted_iota(jnp.int32, shape_w, 0)
    q_w = row_w % 8
    slot_w = jnp.where(q_w < 4, q_w // 2, q_w - 4)
    kind_w = jnp.where(q_w < 4, q_w % 2, jnp.where(q_w < 6, 2, 3))

    def pack(chunk):
        hit = (target == chunk * GROUP + row_w // 8) & (order == slot_w)
        message = jnp.zeros((GROUP * 8, half), F32)
        for kind, part in enumerate(parts):
            picks = jnp.where(hit & (kind_w == kind), 1.0, 0.0).astype(BF16)
            message = message + jnp.dot(picks, part, preferred_element_type=F32)
        send[pl.ds(chunk * GROUP, GROUP)] = message.reshape(GROUP, 8, half).astype(BF16)

    if devices == GROUP:
        pack(0)
    else:
        pl.loop(0, devices // GROUP)(pack)
    recv[me] = send[me]

    pl.semaphore_wait(barrier, devices - 1)

    side = layer // groups
    side_size = devices // 2

    def route(to_layer, to_lat):
        pltpu.make_async_remote_copy(
            src_ref=send.at[to_layer * lateral + to_lat],
            dst_ref=recv.at[me],
            send_sem=send_sem,
            recv_sem=recv_sem.at[side],
            device_id=(to_layer, to_lat),
            device_id_type=MESH,
        ).start()

    def copy(source, target, send_at, recv_at, to, to_lat):
        return pltpu.make_async_remote_copy(
            src_ref=source, dst_ref=target, send_sem=send_at, recv_sem=recv_at,
            device_id=(to, to_lat), device_id_type=MESH,
        )

    partner = layer - step
    onward = layer + 2 * step
    parts_of = [(b, pl.ds(h, half)) for b in reversed(range(blocks)) for h in range(0, r, half)]
    sent = len(parts_of) - 1
    far_copies = [
        copy(
            inv.at[0, b, pl.ds(mine, r), pl.ds(pl.multiple_of(other + h.start, half), half)],
            far.at[b, :, h], far_send.at[i], far_recv.at[i], partner, partner_lat,
        )
        for i, (b, h) in enumerate(parts_of)
    ]
    raw_copies = [
        copy(
            inv.at[0, b, pl.ds(other, r), pl.ds(pl.multiple_of(mine + h.start, half), half)],
            zfar.at[b, :, h], zfar_send.at[i], zfar_recv.at[i], onward, next_lat,
        )
        for i, (b, h) in enumerate(parts_of)
    ]
    comp_copies = [
        copy(
            comp.at[b, :, h], zfar.at[b, :, h],
            zfar_send.at[i], zfar_recv.at[i], onward, next_lat,
        )
        for i, (b, h) in enumerate(parts_of)
    ]

    end = parts_of[-1][1]
    head_copy = copy(
        inv.at[0, 0, pl.ds(other, r), pl.ds(mine, r)], head, head_send, head_recv, onward, next_lat
    )
    tail_copy = copy(
        inv.at[0, 0, pl.ds(mine, r), pl.ds(pl.multiple_of(other + end.start, half), half)],
        tail, tail_send, tail_recv,
        layer - 3 * step, jnp.where(place == 1, lat, twin),
    )

    turned = first & (x == 0)

    @pl.when(jnp.logical_not(turned))
    def _():
        for across in range(lateral):
            route(partner, wrap(lat + across, lateral))

    @pl.when(jnp.where(first, x == 1, jnp.logical_not(last)))
    def _():
        for far_copy in far_copies[:sent]:
            far_copy.start()

    @pl.when(jnp.where(first, x == 1, middle))
    def _():
        for far_copy in far_copies[sent:]:
            far_copy.start()

    def route_far(to_layer, to_lat):
        @pl.when(turned | (to_layer != partner))
        def _():
            route(to_layer, to_lat)

    def downward(i):
        at = jnp.where(turned, layers - 3, layers - 1) - i
        return jnp.where(at < 0, at + layers, at)

    others(route_far, downward, 0, layers - 2)

    @pl.when(first)
    def _():
        for raw_copy in raw_copies:
            raw_copy.start()

    others(route_far, downward, layers - 2, layers)

    @pl.when(middle)
    def _():
        head_copy.start()

    @pl.when(odd & jnp.logical_not(last))
    def _():
        tail_copy.start()

    @pl.when(turned)
    def _():
        for far_copy in far_copies:
            far_copy.start()

    for load in loads:
        load.wait()

    u_copy = copy(
        chalf.at[:, pl.ds(other, r), :], usib, u_send, u_recv, layer, twin
    )

    @pl.when(odd & jnp.logical_not(last))
    def _():
        u_copy.start()

    def step_of(b):
        return chalf[b, pl.ds(other, r), :]

    def compose(i):
        b, h = parts_of[i]
        far_copies[i].wait_recv()
        comp[b, :, h] = jnp.dot(
            step_of(b), far[b, :, h], preferred_element_type=F32
        ).astype(BF16)
        if i < sent:
            comp_copies[i].start()

    @pl.when(middle & (x == 0))
    def _():
        for i in range(2):
            compose(i)

    everyone = pl.ds(0, devices - 1)

    shape_u = (BATCH, 8, half)
    q_u = lax.broadcasted_iota(jnp.int32, shape_u, 1)
    lane = lax.broadcasted_iota(jnp.int32, shape_u, 2)
    s_of, half_of, plane_of, block_of = lane % 8, (lane // 8) % 2, (lane // 16) % 2, lane // 32
    wanted = (((s_of * 2 + plane_of) * blocks + block_of) + 1).astype(F32)
    usable = (q_u < 4) & (q_u % 2 == half_of) & (lane < 64)

    def unpack(begin):
        got = recv[pl.ds(begin, BATCH)].astype(F32)
        named_code = jnp.where(q_u < 2, got[:, 4:5, :], got[:, 5:6, :])
        table = jnp.where(usable & (named_code == wanted), 1.0, 0.0)
        return lax.dot_general(
            table.reshape(BATCH * 8, half).astype(BF16),
            got.reshape(BATCH * 8, half).astype(BF16),
            (((0,), (0,)), ((), ())),
            preferred_element_type=F32,
        )

    def unpack_side(at):
        begin = at * side_size
        if side_size == BATCH:
            return unpack(begin)
        return lax.fori_loop(
            0, side_size // BATCH, lambda i, total: total + unpack(begin + i * BATCH),
            jnp.zeros((half, half), F32),
        )

    near = recv.at[pl.ds(0, side_size - 1)]
    distant = recv.at[pl.ds(0, side_size)]
    pltpu.make_async_copy(near, near, recv_sem.at[side]).wait()
    field = unpack_side(side)
    pltpu.make_async_copy(distant, distant, recv_sem.at[1 - side]).wait()
    field = field + unpack_side(1 - side)

    upper = x == 1
    fields, given = [], []
    for b in range(blocks):
        rows = [field[32 * b + 8 * k : 32 * b + 8 * k + 8] for k in range(4)]
        top = jnp.concatenate(rows[:2], axis=1)
        bottom = jnp.concatenate(rows[2:], axis=1)
        own = jnp.where(upper, top, bottom).astype(BF16)
        away = jnp.where(upper, bottom, top).astype(BF16)
        fields.append((own, away))
        passed = nt(own, chalf[b, pl.ds(mine, r), :]) + nt(away, ohalf[b, pl.ds(mine, r), :])
        give[b] = passed.astype(BF16)
        given.append(passed)

    po_copy = copy(give, po, po_send, po_recv, partner, partner_lat)
    start_copy = copy(
        give, cin, t_send, c_recv, layer - 3 * step, lat if groups == 2 else twin
    )
    q_copy = copy(qout, qin, q_send, q_recv, onward, next_lat)
    far_lat = jnp.where(place == groups - 3, twin, lat)
    c_copies = [
        copy(fout, cin, c_send.at[0], c_recv, onward, twin),
        copy(fout, cin, c_send.at[1], c_recv, layer + 4 * step, far_lat),
    ]
    o_copy = copy(fout, oin, o_send, o_recv, layer + step, jnp.where(odd, twin, lat))
    own_copy = copy(qout, osib, own_send, own_recv, layer, twin)
    both_copy = copy(fout, tin, c_send.at[2], trace_recv, onward, lat)
    hand_copy = copy(comp, usib, u_send, u_recv, layer, twin)
    twin_copy = copy(tout, oin, trace_send, o_recv, layer + step, twin)
    trace_copy = copy(tout, tin, trace_send, trace_recv, layer, twin)

    @pl.when(last)
    def _():
        start_copy.start()

    po_copy.start()

    @pl.when(odd & jnp.logical_not(last))
    def _():
        for far_copy in far_copies[sent:]:
            far_copy.start()

    for b in range(blocks):
        own, away = fields[b]
        owned = nt(own, chalf[b, pl.ds(other, r), :]) + nt(away, ohalf[b, pl.ds(other, r), :])
        base[b] = owned
        qout[b] = owned.astype(BF16)

    @pl.when(first)
    def _():
        q_copy.start()

    @pl.when(odd & jnp.logical_not(last))
    def _():
        own_copy.start()

    for b in range(blocks):
        acc[b] = jnp.where(
            upper,
            jnp.concatenate([given[b], base[b]], axis=1),
            jnp.concatenate([base[b], given[b]], axis=1),
        )

    def settle():
        po_copy.wait_send()
        pltpu.make_async_copy(send.at[everyone], send.at[everyone], send_sem).wait()

    def opposite():
        settle()
        for far_copy in far_copies:
            far_copy.wait_send()
        o_copy.wait_recv()
        for b in range(blocks):
            extra[0, b] = nt(oin[b], ohalf[b])

    @pl.when(first)
    def _():
        po_copy.wait_recv()
        for b in range(blocks):
            fout[b] = (nt(po[b], step_of(b)) + base[b]).astype(BF16)
        o_copy.start()
        for b in range(blocks):
            acc[b] = acc[b] + nt(po[b], chalf[b])
        opposite()

    @pl.when(middle)
    def _():
        @pl.when(x == 1)
        def _():
            for i in range(2):
                compose(i)

        compose(2)
        po_copy.wait_recv()
        for b in range(blocks):
            total = nt(po[b], step_of(b)) + base[b]
            base[b] = total
            qout[b] = total.astype(BF16)
        q_copy.start()
        for i in range(3, len(parts_of)):
            compose(i)

        @pl.when(jnp.logical_not(upper_core))
        def _():
            hand_copy.start()

        @pl.when(jnp.logical_not(upper_core))
        def _():
            own_copy.start()
            c_copies[0].wait_recv()

        @pl.when(upper_core)
        def _():
            hand_copy.wait_recv()
            own_copy.wait_recv()
            both_copy.wait_recv()
            for b in range(blocks):
                tout[b] = (nt(tin[b], usib[b]) + osib[b].astype(F32)).astype(BF16)
            twin_copy.start()
            c_copies[0].wait_recv()
            for b in range(blocks):
                fout[b] = (nt(cin[b], comp[b]) + base[b]).astype(BF16)
            o_copy.start()

        for b in range(blocks):
            trace = nt(cin[b], far[b]) + po[b].astype(F32)
            acc[b] = acc[b] + nt(trace.astype(BF16), chalf[b])
        opposite()

    def steps():
        for i in range(sent):
            comp_copies[i].wait_recv()

        @pl.when(place == 1)
        def _():
            for i in range(sent, len(parts_of)):
                comp_copies[i].wait_recv()

        @pl.when(place > 1)
        def _():
            head_copy.wait_recv()
            tail_copy.wait_recv()
            zfar[0, :, end] = jnp.dot(
                head[...], tail[...], preferred_element_type=F32
            ).astype(BF16)

    @pl.when(last)
    def _():
        for far_copy in far_copies:
            far_copy.wait_recv()
        steps()
        for b in range(blocks):
            comp[b] = jnp.dot(far[b], zfar[b], preferred_element_type=F32).astype(BF16)
        po_copy.wait_recv()
        q_copy.wait_recv()
        rest = []
        for b in range(blocks):
            part = nt(qin[b], far[b]) + po[b].astype(F32)
            rest.append(part)
        settle()
        start_copy.wait_send()
        c_copies[0].wait_recv()
        for b in range(blocks):
            trace = nt(cin[b], comp[b]) + rest[b]
            extra[0, b] = nt(trace.astype(BF16), chalf[b])

    @pl.when(odd & jnp.logical_not(last))
    def _():
        u_copy.wait_recv()
        for i, (b, h) in enumerate(parts_of):
            far_copies[i].wait_recv()
            comp[b, :, h] = jnp.dot(
                usib[b], far[b, :, h], preferred_element_type=F32
            ).astype(BF16)
        po_copy.wait_recv()
        own_copy.wait_recv()
        rest = [nt(po[b], usib[b]) + osib[b].astype(F32) for b in range(blocks)]
        steps()
        q_copy.wait_recv()
        c_copies[0].wait_recv()
        middles = []
        for b in range(blocks):
            between = (nt(cin[b], zfar[b]) + qin[b].astype(F32)).astype(BF16)
            fout[b] = (nt(between, comp[b]) + rest[b]).astype(BF16)
            middles.append(between)
        @pl.when(upper_core)
        def _():
            c_copies[1].start()
            both_copy.start()
            c_copies[0].start()

        @pl.when(jnp.logical_not(upper_core))
        def _():
            c_copies[0].start()
            c_copies[1].start()

        o_copy.start()
        for b in range(blocks):
            tout[b] = (nt(middles[b], far[b]) + po[b].astype(F32)).astype(BF16)
        trace_copy.start()
        trace_copy.wait_recv()
        for b in range(blocks):
            acc[b] = acc[b] + nt(tin[b], chalf[b])
        opposite()

    @pl.when(first)
    def _():
        for comp_copy in comp_copies[sent:]:
            comp_copy.wait_send()

    @pl.when(middle)
    def _():
        head_copy.wait_send()

        @pl.when(upper_core)
        def _():
            twin_copy.wait_send()

        @pl.when(jnp.logical_not(upper_core))
        def _():
            hand_copy.wait_send()
            own_copy.wait_send()

    @pl.when(odd & jnp.logical_not(last) & upper_core)
    def _():
        both_copy.wait_send()

    @pl.when(jnp.logical_not(last | (middle & jnp.logical_not(upper_core))))
    def _():
        o_copy.wait_send()

    @pl.when(jnp.logical_not(odd))
    def _():
        for comp_copy in comp_copies[:sent]:
            comp_copy.wait_send()
        q_copy.wait_send()

    @pl.when(odd & jnp.logical_not(last))
    def _():
        for c_copy in [*c_copies, u_copy, own_copy, trace_copy, tail_copy]:
            c_copy.wait_send()


def body(layers, lateral, inverse, tiles, tile_dest, tile_code):
    devices = layers * lateral
    _, blocks, size, _ = inverse.shape
    r = tiles.shape[1]
    src = 8
    dma = pltpu.SemaphoreType.DMA
    small = (blocks, src, r)
    matrix = pltpu.VMEM((blocks, r, r), BF16)
    vmem = pl.BlockSpec(memory_space=pltpu.VMEM)
    most, final = pl.pallas_call(
        functools.partial(kernel, layers, lateral),
        out_shape=[jax.ShapeDtypeStruct((1, blocks, src, size), F32)] * 2,
        in_specs=[pl.BlockSpec(memory_space=pltpu.HBM)] * 4,
        out_specs=[vmem] * 2,
        scratch_shapes=[
            pltpu.VMEM(tiles.shape, BF16),
            pltpu.VMEM((1, tiles.shape[0]), jnp.int32),
            pltpu.VMEM((1, tiles.shape[0]), jnp.int32),
            pltpu.VMEM((devices, 8, r // 2), BF16),
            pltpu.VMEM((devices, 8, r // 2), BF16),
            pltpu.VMEM((blocks, size, r), BF16),
            pltpu.VMEM((blocks, size, r), BF16),
            matrix, matrix, matrix,
            pltpu.VMEM(small, F32),
        ]
        + [pltpu.VMEM(small, BF16)] * 7
        + [matrix]
        + [pltpu.VMEM(small, BF16)] * 3
        + [pltpu.VMEM((r, r), BF16), pltpu.VMEM((r, r // 2), BF16)]
        + [dma((3,)), dma((2,)), dma, dma((2,))]
        + [dma((2 * blocks,))] * 4
        + [dma] * 3
        + [dma((3,))]
        + [dma] * 15,
        compiler_params=pltpu.CompilerParams(
            collective_id=0, has_side_effects=True, vmem_limit_bytes=48 * 1024 * 1024
        ),
        name="sweep",
    )(
        *(
            pltpu.with_memory_space_constraint(array, pltpu.HBM)
            for array in (inverse, tiles, tile_dest.reshape(1, -1), tile_code.reshape(1, -1))
        )
    )
    return most + final


def solution(mesh):
    in_specs = (
        P("layer", "lat", None, None),
        P(("layer", "lat"), None),
        P(("layer", "lat"), None),
        P(("layer", "lat")),
    )
    out_specs = P("layer", "lat", None, None)
    return jax.shard_map(
        functools.partial(body, mesh.shape["layer"], mesh.shape["lat"]),
        mesh=mesh, in_specs=in_specs, out_specs=out_specs, check_vma=False,
    )
```

```python
import functools

import jax
import jax.numpy as jnp
from jax import lax
from jax.experimental import pallas as pl
from jax.experimental.pallas import tpu as pltpu
from jax.sharding import PartitionSpec as P

MESH = pl.DeviceIdType.MESH
F32 = jnp.float32
BF16 = jnp.bfloat16
GROUP = 32
BATCH = 16


def nt(vectors, matrix):
    return lax.dot_general(vectors, matrix, (((1,), (1,)), ((), ())), preferred_element_type=F32)


def kernel(
    layers, lateral,
    inv, tiles_in, dest_in, code_in, out, extra,
    tiles, dest, code, send, recv, chalf, ohalf, far, zfar, comp, base, give, po, cin, oin, qin, qout, fout, usib, osib, tout, tin, head, tail,
    small_sem, load_sem, send_sem, recv_sem, far_send, far_recv, zfar_send, zfar_recv,
    po_send, po_recv, t_send, c_send, c_recv, o_send, o_recv, q_send, q_recv,
    head_send, head_recv, tail_send, tail_recv, u_send, u_recv, own_send, own_recv, trace_send, trace_recv,
):
    layer = lax.axis_index("layer")
    lat = lax.axis_index("lat")
    devices = layers * lateral
    me = layer * lateral + lat
    x = lax.rem(layer, 2)
    group = layer // 2
    groups = layers // 2
    step = 2 * x - 1
    place = jnp.where(x == 1, group, groups - 1 - group)
    blocks, size, r = chalf.shape
    acc = out.at[0]
    count = tiles.shape[0]
    mine = pl.multiple_of((1 - x) * r, r)
    other = pl.multiple_of(x * r, r)
    first = place == 0
    last = place == groups - 1
    odd = lax.rem(place, 2) == 1
    middle = jnp.logical_not(odd | first)
    twin = lat + 1 - 2 * lax.rem(lat, 2)
    partner_lat = jnp.where(middle, twin, lat)
    upper_core = lax.rem(lat, 2) == 1
    next_lat = jnp.where(place == groups - 2, lat, twin)

    def others(visit, pick, begin, end):
        def visit_layer(i):
            to = pick(i)

            @pl.when(to != layer)
            def _():
                visit(to, lat)

            for across in [*range(2, lateral, 2), *range(1, lateral, 2)]:
                visit(to, wrap(lat + across, lateral))

        if devices == GROUP:
            for i in range(begin, end):
                visit_layer(i)
        else:
            pl.loop(begin, end)(visit_layer)

    def wrap(index, length):
        return jnp.where(index >= length, index - length, index)

    smalls = [
        pltpu.make_async_copy(source, target, small_sem.at[i])
        for i, (source, target) in enumerate(((tiles_in, tiles), (dest_in, dest), (code_in, code)))
    ]
    barrier = pltpu.get_barrier_semaphore()

    def greet(to_layer, to_lat):
        pl.semaphore_signal(
            barrier, inc=1, device_id=(to_layer, to_lat), device_id_type=MESH
        )

    others(greet, lambda i: i, 0, 2)

    for load in smalls:
        load.start()
    loads = [
        pltpu.make_async_copy(inv.at[0, :, :, pl.ds(mine, r)], chalf, load_sem.at[0]),
        pltpu.make_async_copy(inv.at[0, :, :, pl.ds(other, r)], ohalf, load_sem.at[1]),
    ]
    for load in loads:
        load.start()

    others(greet, lambda i: i, 2, layers)

    for load in smalls:
        load.wait()

    row_t = lax.broadcasted_iota(jnp.int32, (count, count), 0)
    col_t = lax.broadcasted_iota(jnp.int32, (count, count), 1)
    target = dest[...]
    across = jnp.broadcast_to(target, (count, count))
    named = jnp.sum(jnp.where(row_t == col_t, across, 0), axis=1, keepdims=True)
    order = jnp.sum(
        jnp.where((named == target) & (row_t < col_t), 1, 0), axis=0, keepdims=True
    )
    codes = jnp.broadcast_to(code[...], (count, count)) + 1
    code_col = jnp.sum(jnp.where(row_t == col_t, codes, 0), axis=1, keepdims=True)
    half = r // 2
    parts = [
        tiles[:, :half],
        tiles[:, half:],
        jnp.broadcast_to(code_col, (count, half)).astype(F32).astype(BF16),
    ]
    shape_w = (GROUP * 8, count)
    row_w = lax.broadcasted_iota(jnp.int32, shape_w, 0)
    q_w = row_w % 8
    slot_w = jnp.where(q_w < 4, q_w // 2, q_w - 4)
    kind_w = jnp.where(q_w < 4, q_w % 2, jnp.where(q_w < 6, 2, 3))

    def pack(chunk):
        hit = (target == chunk * GROUP + row_w // 8) & (order == slot_w)
        message = jnp.zeros((GROUP * 8, half), F32)
        for kind, part in enumerate(parts):
            picks = jnp.where(hit & (kind_w == kind), 1.0, 0.0).astype(BF16)
            message = message + jnp.dot(picks, part, preferred_element_type=F32)
        send[pl.ds(chunk * GROUP, GROUP)] = message.reshape(GROUP, 8, half).astype(BF16)

    if devices == GROUP:
        pack(0)
    else:
        pl.loop(0, devices // GROUP)(pack)
    recv[me] = send[me]

    pl.semaphore_wait(barrier, devices - 1)

    side = layer // groups
    side_size = devices // 2

    def route(to_layer, to_lat):
        pltpu.make_async_remote_copy(
            src_ref=send.at[to_layer * lateral + to_lat],
            dst_ref=recv.at[me],
            send_sem=send_sem,
            recv_sem=recv_sem.at[side],
            device_id=(to_layer, to_lat),
            device_id_type=MESH,
        ).start()

    def copy(source, target, send_at, recv_at, to, to_lat):
        return pltpu.make_async_remote_copy(
            src_ref=source, dst_ref=target, send_sem=send_at, recv_sem=recv_at,
            device_id=(to, to_lat), device_id_type=MESH,
        )

    partner = layer - step
    onward = layer + 2 * step
    parts_of = [(b, pl.ds(h, half)) for b in reversed(range(blocks)) for h in range(0, r, half)]
    sent = len(parts_of) - 1
    far_copies = [
        copy(
            inv.at[0, b, pl.ds(mine, r), pl.ds(pl.multiple_of(other + h.start, half), half)],
            far.at[b, :, h], far_send.at[i], far_recv.at[i], partner, partner_lat,
        )
        for i, (b, h) in enumerate(parts_of)
    ]
    raw_copies = [
        copy(
            inv.at[0, b, pl.ds(other, r), pl.ds(pl.multiple_of(mine + h.start, half), half)],
            zfar.at[b, :, h], zfar_send.at[i], zfar_recv.at[i], onward, next_lat,
        )
        for i, (b, h) in enumerate(parts_of)
    ]
    comp_copies = [
        copy(
            comp.at[b, :, h], zfar.at[b, :, h],
            zfar_send.at[i], zfar_recv.at[i], onward, next_lat,
        )
        for i, (b, h) in enumerate(parts_of)
    ]

    end = parts_of[-1][1]
    head_copy = copy(
        inv.at[0, 0, pl.ds(other, r), pl.ds(mine, r)], head, head_send, head_recv, onward, next_lat
    )
    tail_copy = copy(
        inv.at[0, 0, pl.ds(mine, r), pl.ds(pl.multiple_of(other + end.start, half), half)],
        tail, tail_send, tail_recv,
        layer - 3 * step, jnp.where(place == 1, lat, twin),
    )

    turned = first & (x == 0)

    @pl.when(jnp.logical_not(turned))
    def _():
        for across in range(lateral):
            route(partner, wrap(lat + across, lateral))

    @pl.when(jnp.where(first, x == 1, jnp.logical_not(last)))
    def _():
        for far_copy in far_copies[:sent]:
            far_copy.start()

    @pl.when(jnp.where(first, x == 1, middle))
    def _():
        for far_copy in far_copies[sent:]:
            far_copy.start()

    def route_far(to_layer, to_lat):
        @pl.when(turned | (to_layer != partner))
        def _():
            route(to_layer, to_lat)

    def downward(i):
        at = jnp.where(turned, layers - 3, layers - 1) - i
        return jnp.where(at < 0, at + layers, at)

    others(route_far, downward, 0, layers - 2)

    @pl.when(first)
    def _():
        for raw_copy in raw_copies:
            raw_copy.start()

    others(route_far, downward, layers - 2, layers)

    @pl.when(middle)
    def _():
        head_copy.start()

    @pl.when(odd & jnp.logical_not(last))
    def _():
        tail_copy.start()

    @pl.when(turned)
    def _():
        for far_copy in far_copies:
            far_copy.start()

    for load in loads:
        load.wait()

    u_copy = copy(
        chalf.at[:, pl.ds(other, r), :], usib, u_send, u_recv, layer, twin
    )

    @pl.when(odd & jnp.logical_not(last))
    def _():
        u_copy.start()

    def step_of(b):
        return chalf[b, pl.ds(other, r), :]

    def compose(i):
        b, h = parts_of[i]
        far_copies[i].wait_recv()
        comp[b, :, h] = jnp.dot(
            step_of(b), far[b, :, h], preferred_element_type=F32
        ).astype(BF16)
        if i < sent:
            comp_copies[i].start()

    @pl.when(middle & (x == 0))
    def _():
        for i in range(1):
            compose(i)

    everyone = pl.ds(0, devices - 1)

    shape_u = (BATCH, 8, half)
    q_u = lax.broadcasted_iota(jnp.int32, shape_u, 1)
    lane = lax.broadcasted_iota(jnp.int32, shape_u, 2)
    s_of, half_of, plane_of, block_of = lane % 8, (lane // 8) % 2, (lane // 16) % 2, lane // 32
    wanted = (((s_of * 2 + plane_of) * blocks + block_of) + 1).astype(F32)
    usable = (q_u < 4) & (q_u % 2 == half_of) & (lane < 64)

    def unpack(begin):
        got = recv[pl.ds(begin, BATCH)].astype(F32)
        named_code = jnp.where(q_u < 2, got[:, 4:5, :], got[:, 5:6, :])
        table = jnp.where(usable & (named_code == wanted), 1.0, 0.0)
        return lax.dot_general(
            table.reshape(BATCH * 8, half).astype(BF16),
            got.reshape(BATCH * 8, half).astype(BF16),
            (((0,), (0,)), ((), ())),
            preferred_element_type=F32,
        )

    def unpack_side(at):
        begin = at * side_size
        if side_size == BATCH:
            return unpack(begin)
        return lax.fori_loop(
            0, side_size // BATCH, lambda i, total: total + unpack(begin + i * BATCH),
            jnp.zeros((half, half), F32),
        )

    near = recv.at[pl.ds(0, side_size - 1)]
    distant = recv.at[pl.ds(0, side_size)]
    pltpu.make_async_copy(near, near, recv_sem.at[side]).wait()
    field = unpack_side(side)

    @pl.when(middle & (x == 0))
    def _():
        compose(1)

    pltpu.make_async_copy(distant, distant, recv_sem.at[1 - side]).wait()
    field = field + unpack_side(1 - side)

    upper = x == 1
    fields, given = [], []
    for b in range(blocks):
        rows = [field[32 * b + 8 * k : 32 * b + 8 * k + 8] for k in range(4)]
        top = jnp.concatenate(rows[:2], axis=1)
        bottom = jnp.concatenate(rows[2:], axis=1)
        own = jnp.where(upper, top, bottom).astype(BF16)
        away = jnp.where(upper, bottom, top).astype(BF16)
        fields.append((own, away))
        passed = nt(own, chalf[b, pl.ds(mine, r), :]) + nt(away, ohalf[b, pl.ds(mine, r), :])
        give[b] = passed.astype(BF16)
        given.append(passed)

    po_copy = copy(give, po, po_send, po_recv, partner, partner_lat)
    start_copy = copy(
        give, cin, t_send, c_recv, layer - 3 * step, lat if groups == 2 else twin
    )
    q_copy = copy(qout, qin, q_send, q_recv, onward, next_lat)
    far_lat = jnp.where(place == groups - 3, twin, lat)
    c_copies = [
        copy(fout, cin, c_send.at[0], c_recv, onward, twin),
        copy(fout, cin, c_send.at[1], c_recv, layer + 4 * step, far_lat),
    ]
    o_copy = copy(fout, oin, o_send, o_recv, layer + step, jnp.where(odd, twin, lat))
    own_copy = copy(qout, osib, own_send, own_recv, layer, twin)
    both_copy = copy(fout, tin, c_send.at[2], trace_recv, onward, lat)
    hand_copy = copy(comp, usib, u_send, u_recv, layer, twin)
    twin_copy = copy(tout, oin, trace_send, o_recv, layer + step, twin)
    trace_copy = copy(tout, tin, trace_send, trace_recv, layer, twin)

    @pl.when(last)
    def _():
        start_copy.start()

    po_copy.start()

    @pl.when(odd & jnp.logical_not(last))
    def _():
        for far_copy in far_copies[sent:]:
            far_copy.start()

    for b in range(blocks):
        own, away = fields[b]
        owned = nt(own, chalf[b, pl.ds(other, r), :]) + nt(away, ohalf[b, pl.ds(other, r), :])
        base[b] = owned
        qout[b] = owned.astype(BF16)

    @pl.when(first)
    def _():
        q_copy.start()

    @pl.when(odd & jnp.logical_not(last))
    def _():
        own_copy.start()

    for b in range(blocks):
        acc[b] = jnp.where(
            upper,
            jnp.concatenate([given[b], base[b]], axis=1),
            jnp.concatenate([base[b], given[b]], axis=1),
        )

    def opposite():
        o_copy.wait_recv()
        for b in range(blocks):
            extra[0, b] = nt(oin[b], ohalf[b])

    @pl.when(first)
    def _():
        po_copy.wait_recv()
        for b in range(blocks):
            fout[b] = (nt(po[b], step_of(b)) + base[b]).astype(BF16)
        o_copy.start()
        for b in range(blocks):
            acc[b] = acc[b] + nt(po[b], chalf[b])
        opposite()

    @pl.when(middle)
    def _():
        @pl.when(x == 1)
        def _():
            for i in range(2):
                compose(i)

        compose(2)
        po_copy.wait_recv()
        for b in range(blocks):
            total = nt(po[b], step_of(b)) + base[b]
            base[b] = total
            qout[b] = total.astype(BF16)
        q_copy.start()
        for i in range(3, len(parts_of)):
            compose(i)

        @pl.when(jnp.logical_not(upper_core))
        def _():
            hand_copy.start()

        @pl.when(jnp.logical_not(upper_core))
        def _():
            own_copy.start()
            c_copies[0].wait_recv()

        @pl.when(upper_core)
        def _():
            hand_copy.wait_recv()
            own_copy.wait_recv()
            both_copy.wait_recv()
            for b in range(blocks):
                tout[b] = (nt(tin[b], usib[b]) + osib[b].astype(F32)).astype(BF16)
            twin_copy.start()
            c_copies[0].wait_recv()
            for b in range(blocks):
                fout[b] = (nt(cin[b], comp[b]) + base[b]).astype(BF16)
            o_copy.start()

        for b in range(blocks):
            trace = nt(cin[b], far[b]) + po[b].astype(F32)
            acc[b] = acc[b] + nt(trace.astype(BF16), chalf[b])
        opposite()

    def steps():
        for i in range(sent):
            comp_copies[i].wait_recv()

        @pl.when(place == 1)
        def _():
            for i in range(sent, len(parts_of)):
                comp_copies[i].wait_recv()

        @pl.when(place > 1)
        def _():
            head_copy.wait_recv()
            tail_copy.wait_recv()
            zfar[0, :, end] = jnp.dot(
                head[...], tail[...], preferred_element_type=F32
            ).astype(BF16)

    @pl.when(last)
    def _():
        for far_copy in far_copies:
            far_copy.wait_recv()
        steps()
        for b in range(blocks):
            comp[b] = jnp.dot(far[b], zfar[b], preferred_element_type=F32).astype(BF16)
        po_copy.wait_recv()
        q_copy.wait_recv()
        rest = []
        for b in range(blocks):
            part = nt(qin[b], far[b]) + po[b].astype(F32)
            rest.append(part)
        c_copies[0].wait_recv()
        for b in range(blocks):
            trace = nt(cin[b], comp[b]) + rest[b]
            extra[0, b] = nt(trace.astype(BF16), chalf[b])

    @pl.when(odd & jnp.logical_not(last))
    def _():
        u_copy.wait_recv()
        for i, (b, h) in enumerate(parts_of):
            far_copies[i].wait_recv()
            comp[b, :, h] = jnp.dot(
                usib[b], far[b, :, h], preferred_element_type=F32
            ).astype(BF16)
        po_copy.wait_recv()
        own_copy.wait_recv()
        rest = [nt(po[b], usib[b]) + osib[b].astype(F32) for b in range(blocks)]
        steps()
        q_copy.wait_recv()
        c_copies[0].wait_recv()
        middles = []
        for b in range(blocks):
            between = (nt(cin[b], zfar[b]) + qin[b].astype(F32)).astype(BF16)
            fout[b] = (nt(between, comp[b]) + rest[b]).astype(BF16)
            middles.append(between)
        @pl.when(upper_core)
        def _():
            c_copies[1].start()
            both_copy.start()
            c_copies[0].start()

        @pl.when(jnp.logical_not(upper_core))
        def _():
            c_copies[0].start()
            c_copies[1].start()

        o_copy.start()
        for b in range(blocks):
            tout[b] = (nt(middles[b], far[b]) + po[b].astype(F32)).astype(BF16)
        trace_copy.start()
        trace_copy.wait_recv()
        for b in range(blocks):
            acc[b] = acc[b] + nt(tin[b], chalf[b])
        opposite()

    @pl.when(jnp.logical_not(last))
    def _():
        for far_copy in far_copies:
            far_copy.wait_send()

    @pl.when(last)
    def _():
        start_copy.wait_send()

    @pl.when(first)
    def _():
        for comp_copy in comp_copies[sent:]:
            comp_copy.wait_send()

    @pl.when(middle)
    def _():
        head_copy.wait_send()

        @pl.when(upper_core)
        def _():
            twin_copy.wait_send()

        @pl.when(jnp.logical_not(upper_core))
        def _():
            hand_copy.wait_send()
            own_copy.wait_send()

    @pl.when(odd & jnp.logical_not(last) & upper_core)
    def _():
        both_copy.wait_send()

    @pl.when(jnp.logical_not(last | (middle & jnp.logical_not(upper_core))))
    def _():
        o_copy.wait_send()

    @pl.when(jnp.logical_not(odd))
    def _():
        for comp_copy in comp_copies[:sent]:
            comp_copy.wait_send()
        q_copy.wait_send()

    @pl.when(odd & jnp.logical_not(last))
    def _():
        for c_copy in [*c_copies, u_copy, own_copy, trace_copy, tail_copy]:
            c_copy.wait_send()

    po_copy.wait_send()
    pltpu.make_async_copy(send.at[everyone], send.at[everyone], send_sem).wait()


def body(layers, lateral, inverse, tiles, tile_dest, tile_code):
    devices = layers * lateral
    _, blocks, size, _ = inverse.shape
    r = tiles.shape[1]
    src = 8
    dma = pltpu.SemaphoreType.DMA
    small = (blocks, src, r)
    matrix = pltpu.VMEM((blocks, r, r), BF16)
    vmem = pl.BlockSpec(memory_space=pltpu.VMEM)
    most, final = pl.pallas_call(
        functools.partial(kernel, layers, lateral),
        out_shape=[jax.ShapeDtypeStruct((1, blocks, src, size), F32)] * 2,
        in_specs=[pl.BlockSpec(memory_space=pltpu.HBM)] * 4,
        out_specs=[vmem] * 2,
        scratch_shapes=[
            pltpu.VMEM(tiles.shape, BF16),
            pltpu.VMEM((1, tiles.shape[0]), jnp.int32),
            pltpu.VMEM((1, tiles.shape[0]), jnp.int32),
            pltpu.VMEM((devices, 8, r // 2), BF16),
            pltpu.VMEM((devices, 8, r // 2), BF16),
            pltpu.VMEM((blocks, size, r), BF16),
            pltpu.VMEM((blocks, size, r), BF16),
            matrix, matrix, matrix,
            pltpu.VMEM(small, F32),
        ]
        + [pltpu.VMEM(small, BF16)] * 7
        + [matrix]
        + [pltpu.VMEM(small, BF16)] * 3
        + [pltpu.VMEM((r, r), BF16), pltpu.VMEM((r, r // 2), BF16)]
        + [dma((3,)), dma((2,)), dma, dma((2,))]
        + [dma((2 * blocks,))] * 4
        + [dma] * 3
        + [dma((3,))]
        + [dma] * 15,
        compiler_params=pltpu.CompilerParams(
            collective_id=0, has_side_effects=True, vmem_limit_bytes=48 * 1024 * 1024
        ),
        name="sweep",
    )(
        *(
            pltpu.with_memory_space_constraint(array, pltpu.HBM)
            for array in (inverse, tiles, tile_dest.reshape(1, -1), tile_code.reshape(1, -1))
        )
    )
    return most + final


def solution(mesh):
    in_specs = (
        P("layer", "lat", None, None),
        P(("layer", "lat"), None),
        P(("layer", "lat"), None),
        P(("layer", "lat")),
    )
    out_specs = P("layer", "lat", None, None)
    return jax.shard_map(
        functools.partial(body, mesh.shape["layer"], mesh.shape["lat"]),
        mesh=mesh, in_specs=in_specs, out_specs=out_specs, check_vma=False,
    )
```
